32 devices in a mesh: grp: 2 (over y), wide: 8 (over z, x), narrow: 2 (over core).
Axes of the slice: x: 2, y: 2, z: 4, core: 2. Of those that a mesh axis runs over, the one named last changes fastest.
Arguments:
- denoised: float32 [4, 512, 512], P('grp', 'wide', 'narrow'), parts along dimension 0, may hold values from -6 to 6
- clean_volume: float32 [4, 512, 512], P('grp', 'wide', 'narrow'), parts along dimension 0, may hold values from -6 to 6
- weight: float32 [512, 512], P(('wide', 'narrow')), may hold values from 0.1 to 2
- act_in: bfloat16 [64, 4, 512, 512], P(None, 'grp', 'wide', 'narrow'), parts along dimension 1, may hold values from -6 to 6
- act_mid: bfloat16 [64, 4, 512, 512], P(None, 'grp', 'wide', 'narrow'), parts along dimension 1, as said below
- w_first: bfloat16 [27, 64, 64], replicated, may hold values from -0.15625 to 0.15625
- w_second: bfloat16 [27, 64], replicated, may hold values from -0.15625 to 0.15625
Outputs:
- grad_in: bfloat16 [64, 4, 512, 512], P(None, 'grp', 'wide', 'narrow'), parts along dimension 1
- grad_first: float32 [54, 64, 64], P('grp'), parts along dimension 0
- grad_second: float32 [54, 64], P('grp'), parts along dimension 0
The draws below stay inside these ranges and needn't reach their ends.
There are 2 independent parts, one for each index of `grp`. The reference program is written for one: setup_inputs(seed, part) draws one part's arguments, and reference() takes and returns one part's arrays. A program takes and returns all parts, laid end to end along the dimension named above; an argument that names none is the same for every part. Nothing has to cross between parts.
Inputs may be any that keep to these rules, and one draw needn't show every extreme that they name: act_mid is a rectifier's output: non-negative, with many zeros.
All inputs are finite; a program needn't handle non-finite values.
Results may differ from the reference program's by a relative error of at most 0.0058.
Values may be sent and summed in bfloat16 or wider, within the bound.
No kernel may reach another device: no remote copies, remote signals or barrier semaphores. Data moves between devices by JAX's collectives and lax.ppermute only.
A program may use at most 320 MiB of HBM per device.

```python
import math
import jax
import jax.numpy as jnp

C = 64
NX = 512
NY = 512
NZ = 2


def draw_act_mid(key, part):
    values = jax.random.normal(key, (C, NZ, NX, NY), jnp.float32)
    return jnp.maximum(values, 0.0).astype(jnp.bfloat16)


def block_scale(stream_key, extent, shards, smallest, high):
    def one(position, blocks):
        steps = jax.random.uniform(jax.random.fold_in(jax.random.fold_in(stream_key, 6), position), (blocks,), jnp.float32, smallest / len(shards), high / len(shards))
        return jnp.repeat(jnp.exp(steps), extent[position] // blocks).reshape((-1,) + (1,) * (len(extent) - position - 1))

    gain = one(*shards[0])
    for cut in shards[1:]:
        gain = gain * one(*cut)
    return gain


def bell_draw(own_key, shape, scale, most, cuts=(), held_as=jnp.bfloat16):
    gain = block_scale(own_key, shape, cuts, -0.22, 0.18) if cuts else 1.0
    result = jax.random.normal(own_key, shape, jnp.float32) * scale * gain
    return jnp.minimum(jnp.maximum(result, -most), most).astype(held_as)


def setup_inputs(seed: int = 0, part: int = 0) -> dict:
    streams_of = jax.random.split(jax.random.key(seed), 8)
    part_keys = jax.random.split(jax.random.fold_in(streams_of[7], part), 8)
    denoised = bell_draw(part_keys[0], (NZ, NX, NY), 1.0, 6.0, ((1, 8), (2, 2)), jnp.float32)
    clean_volume = bell_draw(part_keys[1], (NZ, NX, NY), 1.0, 6.0, ((1, 8), (2, 2)), jnp.float32)
    weight = jnp.clip(jnp.exp(math.log(2.0) - 2.9957323 * jax.random.uniform(streams_of[2], (NY, NX), jnp.float32) ** block_scale(streams_of[2], (NY, NX), ((0, 16),), -0.2, 0.2)), 0.1, 2.0)
    act_in = bell_draw(part_keys[3], (C, NZ, NX, NY), 1.0, 6.0, ((2, 8), (3, 2)))
    act_mid = draw_act_mid(jax.random.fold_in(jax.random.fold_in(streams_of[7], part), 71), part)
    w_first = bell_draw(streams_of[5], (27, C, C), (27 * C) ** -0.5, 0.15625)
    w_second = bell_draw(streams_of[6], (27, C), (27 * C) ** -0.5, 0.15625)
    return dict(denoised=denoised, clean_volume=clean_volume, weight=weight, act_in=act_in, act_mid=act_mid, w_first=w_first, w_second=w_second)


def window(padded, tap_index, slices, rows_x, cols_y):
    step_z = tap_index // 9 - 1
    step_x = (tap_index // 3) % 3 - 1
    step_y = tap_index % 3 - 1
    return padded[..., 1 - step_z:1 - step_z + slices, 1 - step_x:1 - step_x + rows_x, 1 - step_y:1 - step_y + cols_y]


def reference(denoised, clean_volume, weight, act_in, act_mid, w_first, w_second):
    slices, rows_x, cols_y = denoised.shape
    error_field = denoised - clean_volume
    spectrum = jnp.fft.fft2(error_field, axes=(1, 2))
    weighted = spectrum * jnp.transpose(weight)[None, :, :]
    field_real = jnp.real(jnp.fft.ifft2(weighted, axes=(1, 2)))
    grad_noise = (-2.0 * field_real).astype(jnp.bfloat16)
    noise_pad = jnp.pad(grad_noise.astype(jnp.float32), 1)
    mid_values = act_mid.astype(jnp.float32)
    second_weights = w_second.astype(jnp.float32)
    grad_mid = jnp.zeros(mid_values.shape, jnp.float32)
    second_rows = []
    for tap_index in range(27):
        shifted = window(noise_pad, tap_index, slices, rows_x, cols_y)
        grad_mid = grad_mid + second_weights[tap_index][:, None, None, None] * shifted[None, :, :, :]
        second_rows.append(jnp.einsum("czxy,zxy->c", mid_values, shifted))
    masked = jnp.where(act_mid > 0, grad_mid, jnp.zeros_like(grad_mid)).astype(jnp.bfloat16)
    masked_pad = jnp.pad(masked.astype(jnp.float32), ((0, 0), (1, 1), (1, 1), (1, 1)))
    in_values = act_in.astype(jnp.float32)
    first_weights = w_first.astype(jnp.float32)
    grad_in = jnp.zeros(in_values.shape, jnp.float32)
    first_rows = []
    for tap_index in range(27):
        shifted = window(masked_pad, tap_index, slices, rows_x, cols_y)
        first_rows.append(jnp.einsum("izxy,ozxy->io", in_values, shifted))
        grad_in = grad_in + jnp.einsum("io,ozxy->izxy", first_weights[tap_index], shifted)
    return grad_in.astype(jnp.bfloat16), jnp.stack(first_rows), jnp.stack(second_rows)
```

```python
import functools

import jax
import jax.numpy as jnp
import ml_dtypes
import numpy as np
from jax import lax
from jax.experimental import pallas as pl
from jax.experimental.pallas import tpu as pltpu
from jax.sharding import PartitionSpec as P

two_pi = 6.283185307179586
highest = lax.Precision.HIGHEST
bf16 = jnp.bfloat16
f32 = jnp.float32


def split_table(table):
    high = table.astype(np.float32).astype(ml_dtypes.bfloat16)
    low = (table - high.astype(np.float64)).astype(np.float32).astype(ml_dtypes.bfloat16)
    return np.stack([high, low])


def cos_sin(left, right, length):
    angles = (np.outer(left, right) % length) * (2.0 * np.pi / length)
    return np.cos(angles), np.sin(angles)


def y_table(wide, keep, half):
    total = 2 * half
    ky = np.arange(total)
    rows = np.zeros(half + 128, np.int64)
    used = np.zeros(half + 128)
    rows[:half] = np.arange(half)
    used[:half] = 1
    for lane, y in ((0, half), (1, half + 1), (127, -1), (126, -2)):
        rows[half + lane] = y
        used[half + lane] = 1
    cos, sin = cos_sin(rows, ky, total)
    cos, sin = cos * used[:, None], -sin * used[:, None]
    shape = (half + 128, wide, 2, keep)
    both = np.stack([cos.reshape(shape), sin.reshape(shape)], axis=2)
    return split_table(both.reshape(half + 128, wide * 4 * keep))


def x_table(total):
    index = np.arange(total)
    cos, sin = cos_sin(index, index, total)
    return split_table(np.concatenate([cos, sin], axis=0))


def dot(a, b):
    return jnp.dot(a, b, preferred_element_type=f32)


def dot_nt(a, b):
    return lax.dot_general(a, b, (((1,), (1,)), ((), ())), preferred_element_type=f32)


def parts_of(x):
    high = x.astype(bf16)
    return high, (x - high.astype(f32)).astype(bf16)


def lanes_of(shape):
    return lax.broadcasted_iota(jnp.int32, shape, len(shape) - 1)


def forward_y_kernel(index_ref, own_ref, other_ref, table_ref, out_ref):
    slices, rows, half = own_ref.shape
    wide = out_ref.shape[0]
    narrow = index_ref[0]
    stacked = jnp.concatenate(
        [own_ref[...].reshape(slices * rows, half), other_ref[...].reshape(slices * rows, half)],
        axis=0,
    )
    high, low = parts_of(stacked)
    t_high = table_ref[0, :half, :]
    t_low = table_ref[1, :half, :]
    total = dot(high, t_high) + dot(low, t_high) + dot(high, t_low)
    lane = lanes_of((1, 128))
    sign = (1 - 2 * (lane % 2)).astype(f32)
    own_scale = jnp.where(narrow == 0, 1.0, sign)
    other_scale = jnp.where(narrow == 0, sign, 1.0)
    first = (lane // 32) % 2 == 0
    count = slices * rows
    for w in range(wide):
        cols = slice(128 * w, 128 * (w + 1))
        merged = total[:count, cols] * own_scale + total[count:, cols] * other_scale
        z0 = merged[:rows]
        z1 = merged[rows:]
        as_zero = jnp.where(first, z0, pltpu.roll(z1, 32, 1))
        as_one = jnp.where(first, pltpu.roll(z0, 96, 1), z1)
        out_ref[w] = jnp.where(narrow == 0, as_zero, as_one)


def forward_y(index, own, other, table, wide):
    slices, rows, half = own.shape
    return pl.pallas_call(
        forward_y_kernel,
        out_shape=jax.ShapeDtypeStruct((wide, rows, 128), f32),
        in_specs=[pl.BlockSpec(memory_space=pltpu.SMEM)] + [pl.BlockSpec(memory_space=pltpu.VMEM)] * 3,
        out_specs=pl.BlockSpec(memory_space=pltpu.VMEM),
        compiler_params=pltpu.CompilerParams(vmem_limit_bytes=40 << 20),
        name="forward_y",
    )(index, own, other, table)


def along_x_kernel(in_ref, table_ref, weight_ref, out_ref, line_ref):
    wide, rows, lanes = in_ref.shape
    total = wide * rows
    held = out_ref.shape[1]
    lane = lanes_of((1, lanes))
    sign = jnp.where(lane < 64, 1.0, -1.0)
    t_high = table_ref[0]
    t_low = table_ref[1]

    def transform(value):
        high, low = parts_of(value)
        both = dot(t_high, jnp.concatenate([high, low], axis=1))
        return both[:, :lanes] + both[:, lanes:] + dot(t_low, high)

    spread = transform(in_ref[...].reshape(total, lanes))
    spectrum = spread[:total] + sign * pltpu.roll(spread[total:], 64, 1)
    back = transform(spectrum * weight_ref[...])
    line_ref[:8] = jnp.zeros((8, lanes), f32)
    line_ref[8 + total :] = jnp.zeros((8, lanes), f32)
    line_ref[8 : 8 + total] = back[:total] - sign * pltpu.roll(back[total:], 64, 1)
    for w in range(wide):
        out_ref[w] = line_ref[6 + rows * w : 6 + rows * w + held]


def along_x(pieces, table, weight_lines):
    wide, rows, lanes = pieces.shape
    return pl.pallas_call(
        along_x_kernel,
        out_shape=jax.ShapeDtypeStruct((wide, rows + 8, lanes), f32),
        in_specs=[pl.BlockSpec(memory_space=pltpu.VMEM)] * 3,
        out_specs=pl.BlockSpec(memory_space=pltpu.VMEM),
        scratch_shapes=[pltpu.VMEM((wide * rows + 16, lanes), f32)],
        compiler_params=pltpu.CompilerParams(vmem_limit_bytes=40 << 20),
        name="along_x",
    )(pieces, table, weight_lines)


def masked_kernel(
    scale,
    index_ref,
    own_ref,
    other_ref,
    table_ref,
    taps_ref,
    pick_ref,
    top_ref,
    bottom_ref,
    in_hbm,
    mid_hbm,
    side_hbm,
    shifted_hbm,
    pay_ref,
    noise_ref,
    in_ref,
    mid_ref,
    side_ref,
    shifted_ref,
    sum_ref,
    second_ref,
    sems,
):
    wide, held, lanes = own_ref.shape
    rows = held - 8
    groups = rows // 8
    half = mid_ref.shape[1]
    ext = half + 128
    narrow = index_ref[0]
    copies = [
        pltpu.make_async_copy(mid_hbm, mid_ref, sems.at[0]),
        pltpu.make_async_copy(side_hbm, side_ref, sems.at[1]),
        pltpu.make_async_copy(in_hbm, in_ref, sems.at[2]),
    ]
    for copy in copies:
        copy.start()

    lane = lanes_of((1, lanes))
    sign = jnp.where(narrow == 0, 1.0, (1 - 2 * (lane % 2)).astype(f32))
    first = (lane // 32) % 2 == 0
    z_lines = ([], [])
    for w in range(wide):
        own = own_ref[w] * sign
        other = other_ref[w] * sign
        even = jnp.where(narrow == 0, own, other)
        odd = jnp.where(narrow == 0, other, own)
        z_lines[0].append(jnp.where(first, even, pltpu.roll(odd, 32, 1)))
        z_lines[1].append(jnp.where(first, pltpu.roll(even, 96, 1), odd))
    lines = jnp.concatenate(
        [jnp.concatenate(z_lines[0], axis=1), jnp.concatenate(z_lines[1], axis=1)], axis=0
    )
    high, low = parts_of(lines)
    noise = dot_nt(high, table_ref[0]) + dot_nt(low, table_ref[0]) + dot_nt(high, table_ref[1])
    column = lanes_of((1, ext))
    beside = jnp.where(narrow == 0, column - half, ext - 1 - column) < 2
    ours = (column < half) | beside
    noise = jnp.where(ours, noise * scale, 0.0).astype(bf16).astype(f32)
    for d in range(3):
        moved = noise if d == 1 else pltpu.roll(noise, (d - 1) % ext, 1)
        for z in range(2):
            noise_ref[d, z] = moved[z * held : (z + 1) * held]

    copies[0].wait()
    copies[1].wait()
    side_ok = lane == jnp.where(narrow == 0, 0, 127)

    def window_of(start):
        pieces = [noise_ref[d, z, pl.ds(start, 16), :] for z in range(2) for d in range(3)]
        return jnp.concatenate(pieces + [jnp.zeros((32, ext), f32)], axis=0)

    def store_row(window, tap_row, mask, side, row):
        value = dot(taps_ref[pl.ds(tap_row * 128, 128), :], window)
        main = jnp.where(mask.astype(f32) > 0, value[:, :half], 0.0)
        edge = jnp.where((side.astype(f32) > 0) & side_ok, value[:, half:], 0.0)
        whole = jnp.concatenate([main, edge], axis=1)
        where = pl.ds(pl.multiple_of(row * 128, 128), 128)
        for d in range(3):
            moved = whole if d == 1 else pltpu.roll(whole, (d - 1) % ext, 1)
            shifted_ref[d, where, :] = moved[:, :half].astype(bf16)

    second_ref[...] = jnp.zeros_like(second_ref)

    def group_body(g, carry):
        start = pl.multiple_of(g * 8, 8)
        wide_window = window_of(start)
        window = wide_window.astype(bf16)
        turned = wide_window[:, :half].T.astype(bf16)
        here = pl.ds(pl.multiple_of(g * 1024, 1024), 1024)
        second_ref[...] += dot(mid_ref[here, :], turned)
        for m in range(8):
            spot = pl.ds(pl.multiple_of(g * 1024 + m * 128, 128), 128)
            store_row(window, m + 1, mid_ref[spot, :], side_ref[spot, :], g * 8 + m + 1)
        return carry

    lax.fori_loop(0, groups, group_body, 0)
    window = window_of(0).astype(bf16)
    store_row(window, 0, top_ref[:, :half], top_ref[:, half:], 0)
    window = window_of(rows - 8).astype(bf16)
    store_row(window, 9, bottom_ref[:, :half], bottom_ref[:, half:], rows + 1)
    outs = [
        pltpu.make_async_copy(shifted_ref.at[d], shifted_hbm.at[d], sems.at[3 + d])
        for d in range(3)
    ]
    for copy in outs:
        copy.start()

    copies[2].wait()
    sum_ref[...] = jnp.zeros_like(sum_ref)

    def chunk_body(k, carry):
        right = in_ref[pl.ds(pl.multiple_of(k * 4 * half, 4 * half), 4 * half), :]
        for d in range(3):
            left = jnp.concatenate(
                [
                    shifted_ref[d, pl.ds(pl.multiple_of(k * 1024 + 256 * q, 256), 512), :]
                    for q in range(4)
                ],
                axis=1,
            )
            sum_ref[d] += dot(left, right)
        return carry

    lax.fori_loop(0, groups, chunk_body, 0)

    singles = []
    for d in range(3):
        for dx in range(3):
            total = None
            for par in range(2):
                i4 = par + 2 - dx
                block = sum_ref[d, i4 * 128 : (i4 + 1) * 128, par * 128 : (par + 1) * 128]
                total = block if total is None else total + block
            turned = total.T
            upper = turned[:64]
            lower = turned[64:]
            slot = d * 3 + dx
            pay_ref[slot * 64 : (slot + 1) * 64] = jnp.where(lane < 64, lower, upper)
            singles.append(upper + pltpu.roll(lower, 64, 1))
    pieces = [
        second_ref[(m * 2 + z) * 64 : (m * 2 + z + 1) * 64, :] for m in range(8) for z in range(2)
    ]
    second = jnp.dot(
        jnp.concatenate(pieces, axis=1), pick_ref[...], preferred_element_type=f32, precision=highest
    )
    singles.append(second)
    for k in range(5):
        pay_ref[(9 + k) * 64 : (10 + k) * 64] = jnp.where(
            lane < 64, singles[2 * k], pltpu.roll(singles[2 * k + 1], 64, 1)
        )
    for copy in outs:
        copy.wait()


def masked_and_kernels(index, own, other, table, taps, pick, top, bottom, lines_in, mid, side, scale):
    wide, held, lanes = own.shape
    rows = held - 8
    half = mid.shape[1]
    ext = half + 128
    vmem = pl.BlockSpec(memory_space=pltpu.VMEM)
    anywhere = pl.BlockSpec(memory_space=pl.ANY)
    return pl.pallas_call(
        functools.partial(masked_kernel, scale),
        out_shape=(
            jax.ShapeDtypeStruct((3, (rows + 2) * 128, half), bf16),
            jax.ShapeDtypeStruct((14 * 64, 128), f32),
        ),
        in_specs=[pl.BlockSpec(memory_space=pltpu.SMEM)] + [vmem] * 7 + [anywhere] * 3,
        out_specs=(anywhere, vmem),
        scratch_shapes=[
            pltpu.VMEM((3, 2, held, ext), f32),
            pltpu.VMEM(lines_in.shape, bf16),
            pltpu.VMEM(mid.shape, bf16),
            pltpu.VMEM(side.shape, bf16),
            pltpu.VMEM((3, (rows + 2) * 128, half), bf16),
            pltpu.VMEM((3, 512, 256), f32),
            pltpu.VMEM((1024, 128), f32),
            pltpu.SemaphoreType.DMA((6,)),
        ],
        compiler_params=pltpu.CompilerParams(vmem_limit_bytes=56 << 20),
        name="masked_and_kernels",
    )(index, own, other, table, taps, pick, top, bottom, lines_in, mid, side)


def input_kernel(shifted_hbm, weight_ref, out_hbm, shifted_ref, out_ref, in_sems, out_sems):
    rows = out_ref.shape[0] // 128
    groups = rows // 8
    chunk = 8 * 128
    copies = []
    for g in range(groups):
        first = 0 if g == 0 else chunk * g + 256
        last = chunk * (g + 1) + 256
        copies.append(
            [
                pltpu.make_async_copy(
                    shifted_hbm.at[d, first:last], shifted_ref.at[d, first:last], in_sems.at[g, d]
                )
                for d in range(3)
            ]
        )
    for group in copies:
        for copy in group:
            copy.start()
    outs = []
    for g in range(groups):
        for copy in copies[g]:
            copy.wait()

        def pair(q, carry, g=g):
            row = pl.multiple_of(g * chunk + q * 256, 256)
            stacked = jnp.concatenate(
                [shifted_ref[d, pl.ds(row, 512), :] for d in range(3)], axis=0
            )
            out_ref[pl.ds(row, 256), :] = dot(weight_ref[...], stacked).astype(bf16)
            return carry

        lax.fori_loop(0, 4, pair, 0)
        span = slice(g * chunk, (g + 1) * chunk)
        copy = pltpu.make_async_copy(out_ref.at[span], out_hbm.at[span], out_sems.at[g])
        copy.start()
        outs.append(copy)
    for copy in outs:
        copy.wait()


def input_gradient(shifted, weight):
    taps, count, half = shifted.shape
    rows = count // 128 - 2
    anywhere = pl.BlockSpec(memory_space=pl.ANY)
    return pl.pallas_call(
        input_kernel,
        out_shape=jax.ShapeDtypeStruct((rows * 128, half), bf16),
        in_specs=[anywhere, pl.BlockSpec(memory_space=pltpu.VMEM)],
        out_specs=anywhere,
        scratch_shapes=[
            pltpu.VMEM(shifted.shape, bf16),
            pltpu.VMEM((rows * 128, half), bf16),
            pltpu.SemaphoreType.DMA((rows // 8, 3)),
            pltpu.SemaphoreType.DMA((rows // 8,)),
        ],
        cost_estimate=pl.CostEstimate(
            flops=2 * rows * 128 * half * 1536, bytes_accessed=4 * rows * 128 * half * 2, transcendentals=0
        ),
        compiler_params=pltpu.CompilerParams(vmem_limit_bytes=40 << 20),
        name="input_gradient",
    )(shifted, weight)


def tap_choice():
    choice = np.zeros((27, 10, 2, 128), np.float32)
    for dz in (-1, 0, 1):
        for dx in (-1, 0, 1):
            for dy in (-1, 0, 1):
                tap = (dz + 1) * 9 + (dx + 1) * 3 + dy + 1
                for m in range(-1, 9):
                    for z in range(2):
                        if 0 <= z - dz < 2:
                            r = m + 2 - dx
                            choice[tap, m + 1, z, ((z - dz) * 3 + dy + 1) * 16 + r] = 1
    return choice


def kernel_matrix(w_first):
    channels = w_first.shape[1]
    w = w_first.reshape(3, 3, 3, channels, channels)
    grid = jnp.stack([jnp.stack([w[1], w[0]]), jnp.stack([w[2], w[1]])])
    grid = grid.transpose(2, 3, 0, 4, 1, 5).reshape(3, 3, 128, 128)
    none = jnp.zeros((3, 128, 128), w.dtype)
    row0 = jnp.stack([grid[2], grid[1], grid[0], none], axis=2)
    row1 = jnp.stack([none, grid[2], grid[1], grid[0]], axis=2)
    both = jnp.stack([row0, row1])
    return both.transpose(0, 2, 1, 3, 4).reshape(256, 1536)


def fast(denoised, clean_volume, weight, act_in, act_mid, w_first, w_second):
    wide = lax.axis_size("wide")
    slices, rows, half = denoised.shape
    channels = act_in.shape[0]
    keep = weight.shape[0]
    total_x = wide * rows
    total_y = 2 * half
    narrow = lax.axis_index("narrow")
    index = narrow.astype(jnp.int32).reshape(1)
    swap = [(0, 1), (1, 0)]
    table_y = jnp.asarray(y_table(wide, keep, half))
    table_x = jnp.asarray(x_table(total_x))

    error = denoised - clean_volume
    error_other = lax.ppermute(error, "narrow", swap)
    lines = forward_y(index, error, error_other, table_y, wide)
    lines = lax.all_to_all(lines, "wide", 0, 0, tiled=True)

    mid = act_mid.transpose(2, 1, 0, 3).reshape(rows * 128, half)
    edge = jnp.where(narrow == 0, act_mid[..., half - 128 :], act_mid[..., :128])
    side = lax.ppermute(edge, "narrow", swap).transpose(2, 1, 0, 3).reshape(rows * 128, 128)
    first = jnp.concatenate([mid[:128], side[:128]], axis=1)
    last = jnp.concatenate([mid[-128:], side[-128:]], axis=1)
    up = [(i, i + 1) for i in range(wide - 1)]
    top = lax.ppermute(last, "wide", up)
    bottom = lax.ppermute(first, "wide", [(j, i) for i, j in up])
    lines_in = act_in.reshape(channels, slices, rows // 2, 2, half)
    lines_in = lines_in.transpose(2, 4, 3, 1, 0).reshape(rows // 2 * half, 256)

    weight_lines = jnp.tile(weight.T, (1, 4))
    lines = along_x(lines, table_x, weight_lines)
    lines = lax.all_to_all(lines, "wide", 0, 0, tiled=True)
    lines_other = lax.ppermute(lines, "narrow", swap)

    choice = tap_choice()
    taps = jnp.einsum(
        "tc,tmzk->mzck", w_second, jnp.asarray(choice, bf16), preferred_element_type=f32
    )
    taps = taps.astype(bf16).reshape(1280, 128)
    pick = np.zeros((16 * 128, 128), np.float32)
    pick[:, :27] = choice[:, 1:9].reshape(27, 16 * 128).T
    shifted, pay = masked_and_kernels(
        index,
        lines,
        lines_other,
        table_y,
        taps,
        jnp.asarray(pick),
        top,
        bottom,
        lines_in,
        mid,
        side,
        -2.0 / (total_x * total_y),
    )
    grad_in = input_gradient(shifted, kernel_matrix(w_first))
    grad_in = grad_in.reshape(rows, slices, channels, half).transpose(2, 1, 0, 3)

    count = pay.shape[0] // 2
    mine = lax.dynamic_slice_in_dim(pay, narrow * count, count, 0)
    theirs = lax.dynamic_slice_in_dim(pay, (1 - narrow) * count, count, 0)
    mine = mine + lax.ppermute(theirs, "narrow", swap)
    mine = mine.reshape(wide, count // wide, 128)
    mine = lax.all_to_all(mine, "wide", 0, 0, tiled=True)
    mine = jnp.broadcast_to(mine.sum(axis=0, keepdims=True), mine.shape)
    mine = lax.all_to_all(mine, "wide", 0, 0, tiled=True).reshape(count, 128)
    theirs = lax.ppermute(mine, "narrow", swap)
    pay = jnp.concatenate(
        [jnp.where(narrow == 0, mine, theirs), jnp.where(narrow == 0, theirs, mine)], axis=0
    )
    pay = pay.reshape(14, 64, 2, 64)
    outer = pay[:9].reshape(3, 3, 64, 2, 64)
    inner = pay[9:].transpose(0, 2, 1, 3).reshape(10, 64, 64)
    grad_second = inner[9, :, :27].T
    inner = inner[:9].reshape(3, 3, 64, 64)
    grad_first = jnp.stack([outer[:, :, :, 1], inner, outer[:, :, :, 0]])
    grad_first = grad_first.transpose(0, 2, 1, 3, 4).reshape(27, channels, channels)
    return (grad_in, grad_first, grad_second)


def with_halo(x, sides, width):
    for axis, dim in sides:
        devices, length = (lax.axis_size(axis), x.shape[dim])
        up = [(i, (i + 1) % devices) for i in range(devices - 1)]
        down = [(j, i) for i, j in up]
        last = lax.slice_in_dim(x, length - width, length, axis=dim)
        first = lax.slice_in_dim(x, 0, width, axis=dim)
        before = lax.ppermute(last, axis, up)
        after = lax.ppermute(first, axis, down)
        x = jnp.concatenate([before, x, after], axis=dim)
    return x


def phase_table(left_index, right_index, length):
    product = left_index[:, None] * right_index[None, :] % length
    angles = product.astype(jnp.float32) * (two_pi / length)
    return (jnp.cos(angles), jnp.sin(angles))


def shifted_windows(padded, slices, rows_x, cols_y, taps_list):
    windows = []
    for tap_index in taps_list:
        step_z = tap_index // 9 - 1
        step_x = tap_index // 3 % 3 - 1
        step_y = tap_index % 3 - 1
        windows.append(
            padded[
                ...,
                1 - step_z : 1 - step_z + slices,
                1 - step_x : 1 - step_x + rows_x,
                1 - step_y : 1 - step_y + cols_y,
            ]
        )
    return jnp.stack(windows, axis=0)


def plain(denoised, clean_volume, weight, act_in, act_mid, w_first, w_second):
    wide_count = lax.axis_size("wide")
    narrow_count = lax.axis_size("narrow")
    slices, rows_x, half_cols = denoised.shape
    total_y = half_cols * narrow_count
    total_x = rows_x * wide_count
    kept_cols = half_cols // wide_count
    narrow_index = lax.axis_index("narrow")
    error_field = denoised - clean_volume
    columns = lax.iota(jnp.int32, total_y)
    frequency = (
        columns % half_cols // kept_cols * narrow_count + columns // half_cols
    ) * kept_cols + columns % kept_cols
    own_rows = narrow_index * half_cols + lax.iota(jnp.int32, half_cols)
    cos_y, sin_y = phase_table(own_rows, frequency, total_y)
    part_real = jnp.einsum("zxy,yc->zxc", error_field, cos_y, precision=highest)
    part_imag = -jnp.einsum("zxy,yc->zxc", error_field, sin_y, precision=highest)
    spec_real, spec_imag = (
        lax.psum_scatter(part_real, "narrow", scatter_dimension=2, tiled=True),
        lax.psum_scatter(part_imag, "narrow", scatter_dimension=2, tiled=True),
    )
    positions = lax.iota(jnp.int32, total_x)
    cos_x, sin_x = phase_table(positions, positions, total_x)
    pieces = (
        lax.all_to_all(
            spec_real.reshape(slices, rows_x, wide_count, kept_cols),
            "wide",
            split_axis=2,
            concat_axis=1,
            tiled=True,
        ),
        lax.all_to_all(
            spec_imag.reshape(slices, rows_x, wide_count, kept_cols),
            "wide",
            split_axis=2,
            concat_axis=1,
            tiled=True,
        ),
    )
    item_count = pieces[0].shape[0]
    in_real = pieces[0].reshape(item_count, total_x, kept_cols)
    in_imag = pieces[1].reshape(item_count, total_x, kept_cols)
    four_real = jnp.einsum("mxk,xq->mkq", in_real, cos_x, precision=highest) + jnp.einsum(
        "mxk,xq->mkq", in_imag, sin_x, precision=highest
    )
    four_imag = jnp.einsum("mxk,xq->mkq", in_imag, cos_x, precision=highest) - jnp.einsum(
        "mxk,xq->mkq", in_real, sin_x, precision=highest
    )
    weighted_real = weight * four_real
    weighted_imag = weight * four_imag
    out_real = jnp.einsum("mkq,qx->mxk", weighted_real, cos_x, precision=highest) - jnp.einsum(
        "mkq,qx->mxk", weighted_imag, sin_x, precision=highest
    )
    out_imag = jnp.einsum("mkq,qx->mxk", weighted_imag, cos_x, precision=highest) + jnp.einsum(
        "mkq,qx->mxk", weighted_real, sin_x, precision=highest
    )
    back_real = lax.all_to_all(
        out_real.reshape(item_count, wide_count, rows_x, kept_cols),
        "wide",
        split_axis=1,
        concat_axis=3,
        tiled=True,
    ).reshape(item_count, rows_x, half_cols)
    back_imag = lax.all_to_all(
        out_imag.reshape(item_count, wide_count, rows_x, kept_cols),
        "wide",
        split_axis=1,
        concat_axis=3,
        tiled=True,
    ).reshape(item_count, rows_x, half_cols)
    local_cols = lax.iota(jnp.int32, half_cols)
    own_freq = (
        local_cols // kept_cols * narrow_count + narrow_index
    ) * kept_cols + local_cols % kept_cols
    cos_back, sin_back = phase_table(own_freq, columns, total_y)
    part_term = jnp.einsum("zxc,cy->zxy", back_real, cos_back, precision=highest) - jnp.einsum(
        "zxc,cy->zxy", back_imag, sin_back, precision=highest
    )
    field_real = lax.psum_scatter(part_term, "narrow", scatter_dimension=2, tiled=True)
    grad_noise = (field_real * (-2.0 / (total_x * total_y))).astype(jnp.bfloat16)
    noise_rim = with_halo(grad_noise, (("wide", 1), ("narrow", 2)), 1)
    noise_pad = jnp.pad(noise_rim, ((1, 1), (0, 0), (0, 0)))
    noise_windows = shifted_windows(noise_pad, slices, rows_x, half_cols, range(27))
    grad_mid = jnp.einsum(
        "tc,tzxy->czxy", w_second, noise_windows, preferred_element_type=jnp.float32
    )
    masked = jnp.where(act_mid > 0, grad_mid, 0.0).astype(jnp.bfloat16)
    masked_rim = with_halo(masked, (("wide", 2), ("narrow", 3)), 1)
    grad_second = jnp.einsum(
        "czxy,tzxy->tc", act_mid, noise_windows, preferred_element_type=jnp.float32
    )
    masked_pad = jnp.pad(masked_rim, ((0, 0), (1, 1), (0, 0), (0, 0)))
    channels = act_in.shape[0]
    grad_in = jnp.zeros(act_in.shape, jnp.float32)
    first_parts = []
    for plane_index in range(9):
        stacked = shifted_windows(
            masked_pad, slices, rows_x, half_cols, [plane_index, plane_index + 9, plane_index + 18]
        )
        first_parts.append(
            jnp.einsum("izxy,dozxy->dio", act_in, stacked, preferred_element_type=jnp.float32)
        )
        grad_in = grad_in + jnp.einsum(
            "dio,dozxy->izxy", w_first[plane_index::9], stacked, preferred_element_type=jnp.float32
        )
    grad_first = jnp.stack(first_parts, axis=1).reshape(27, channels, channels)
    grad_first, grad_second = lax.psum((grad_first, grad_second), ("wide", "narrow"))
    return (grad_in.astype(jnp.bfloat16), grad_first, grad_second)


def shards(denoised, clean_volume, weight, act_in, act_mid, w_first, w_second):
    sizes = (
        lax.axis_size("wide"),
        lax.axis_size("narrow"),
        *denoised.shape,
        weight.shape[0],
        act_in.shape[0],
    )
    chosen = fast if sizes == (8, 2, 2, 64, 256, 32, 64) else plain
    return chosen(denoised, clean_volume, weight, act_in, act_mid, w_first, w_second)


def solution(mesh):
    placed = (
        P("grp", "wide", "narrow"),
        P("grp", "wide", "narrow"),
        P(("wide", "narrow"), None),
        P(None, "grp", "wide", "narrow"),
        P(None, "grp", "wide", "narrow"),
        P(),
        P(),
    )
    return jax.shard_map(
        shards,
        mesh=mesh,
        in_specs=placed,
        out_specs=(P(None, "grp", "wide", "narrow"), P("grp", None, None), P("grp", None)),
        check_vma=False,
    )
```

```python
import functools

import jax
import jax.numpy as jnp
import ml_dtypes
import numpy as np
from jax import lax
from jax.experimental import pallas as pl
from jax.experimental.pallas import tpu as pltpu
from jax.sharding import PartitionSpec as P

two_pi = 6.283185307179586
highest = lax.Precision.HIGHEST
bf16 = jnp.bfloat16
f32 = jnp.float32


def split_table(table):
    high = table.astype(np.float32).astype(ml_dtypes.bfloat16)
    low = (table - high.astype(np.float64)).astype(np.float32).astype(ml_dtypes.bfloat16)
    return np.stack([high, low])


def cos_sin(left, right, length):
    angles = (np.outer(left, right) % length) * (2.0 * np.pi / length)
    return np.cos(angles), np.sin(angles)


def y_table(wide, keep, half):
    total = 2 * half
    ky = np.arange(total)
    rows = np.zeros(half + 128, np.int64)
    used = np.zeros(half + 128)
    rows[:half] = np.arange(half)
    used[:half] = 1
    for lane, y in ((0, half), (1, half + 1), (127, -1), (126, -2)):
        rows[half + lane] = y
        used[half + lane] = 1
    cos, sin = cos_sin(rows, ky, total)
    cos, sin = cos * used[:, None], -sin * used[:, None]
    shape = (half + 128, wide, 2, keep)
    both = np.stack([cos.reshape(shape), sin.reshape(shape)], axis=2)
    table = split_table(both.reshape(half + 128, wide * 4 * keep))
    return table[:, :half], table[:, half:]


def x_table(total):
    index = np.arange(total)
    cos, sin = cos_sin(index, index, total)
    return split_table(np.concatenate([cos, sin], axis=0))


def dot(a, b):
    return jnp.dot(a, b, preferred_element_type=f32)


def dot_nt(a, b):
    return lax.dot_general(a, b, (((1,), (1,)), ((), ())), preferred_element_type=f32)


def parts_of(x):
    high = x.astype(bf16)
    return high, (x - high.astype(f32)).astype(bf16)


def lanes_of(shape):
    return lax.broadcasted_iota(jnp.int32, shape, len(shape) - 1)


def on_chip(x):
    return pltpu.with_memory_space_constraint(x, pltpu.VMEM)


def off_chip(x):
    return pltpu.with_memory_space_constraint(x, pltpu.HBM)


def forward_y_kernel(index_ref, own_ref, other_ref, table_ref, out_ref):
    slices, rows, half = own_ref.shape
    wide = out_ref.shape[0]
    narrow = index_ref[0]
    stacked = jnp.concatenate(
        [own_ref[...].reshape(slices * rows, half), other_ref[...].reshape(slices * rows, half)],
        axis=0,
    )
    high, low = parts_of(stacked)
    t_high = table_ref[0]
    t_low = table_ref[1]
    total = dot(high, t_high) + dot(low, t_high) + dot(high, t_low)
    lane = lanes_of((1, 128))
    sign = (1 - 2 * (lane % 2)).astype(f32)
    own_scale = jnp.where(narrow == 0, 1.0, sign)
    other_scale = jnp.where(narrow == 0, sign, 1.0)
    first = (lane // 32) % 2 == 0
    count = slices * rows
    for w in range(wide):
        cols = slice(128 * w, 128 * (w + 1))
        merged = total[:count, cols] * own_scale + total[count:, cols] * other_scale
        z0 = merged[:rows]
        z1 = merged[rows:]
        as_zero = jnp.where(first, z0, pltpu.roll(z1, 32, 1))
        as_one = jnp.where(first, pltpu.roll(z0, 96, 1), z1)
        out_ref[w] = jnp.where(narrow == 0, as_zero, as_one)


def forward_y(index, own, other, table, wide):
    slices, rows, half = own.shape
    return pl.pallas_call(
        forward_y_kernel,
        out_shape=jax.ShapeDtypeStruct((wide, rows, 128), f32),
        in_specs=[pl.BlockSpec(memory_space=pltpu.SMEM)] + [pl.BlockSpec(memory_space=pltpu.VMEM)] * 3,
        out_specs=pl.BlockSpec(memory_space=pltpu.VMEM),
        compiler_params=pltpu.CompilerParams(vmem_limit_bytes=10 << 20),
        name="forward_y",
    )(index, own, other, off_chip(table))


def along_x_kernel(in_ref, table_ref, weight_ref, out_ref, line_ref):
    wide, rows, lanes = in_ref.shape
    total = wide * rows
    held = out_ref.shape[1]
    lane = lanes_of((1, lanes))
    sign = jnp.where(lane < 64, 1.0, -1.0)
    t_high = table_ref[0]
    t_low = table_ref[1]

    def transform(value):
        high, low = parts_of(value)
        both = dot(t_high, jnp.concatenate([high, low], axis=1))
        return both[:, :lanes] + both[:, lanes:] + dot(t_low, high)

    spread = transform(in_ref[...].reshape(total, lanes))
    spectrum = spread[:total] + sign * pltpu.roll(spread[total:], 64, 1)
    back = transform(spectrum * weight_ref[...])
    line_ref[:8] = jnp.zeros((8, lanes), f32)
    line_ref[8 + total :] = jnp.zeros((8, lanes), f32)
    line_ref[8 : 8 + total] = back[:total] - sign * pltpu.roll(back[total:], 64, 1)
    for w in range(wide):
        out_ref[w] = line_ref[6 + rows * w : 6 + rows * w + held].astype(out_ref.dtype)


def along_x(pieces, table, weight_lines):
    wide, rows, lanes = pieces.shape
    return pl.pallas_call(
        along_x_kernel,
        out_shape=jax.ShapeDtypeStruct((wide, rows + 8, lanes), bf16),
        in_specs=[pl.BlockSpec(memory_space=pltpu.VMEM)] * 3,
        out_specs=pl.BlockSpec(memory_space=pltpu.VMEM),
        scratch_shapes=[pltpu.VMEM((wide * rows + 16, lanes), f32)],
        compiler_params=pltpu.CompilerParams(vmem_limit_bytes=12 << 20),
        name="along_x",
    )(pieces, table, weight_lines)


def turn_mid_kernel(
    index_ref, whole, other, out_hbm, sent_ref, into, side, sems, last_ref, last_sem, out_ref, out_sems
):
    channels, slices, rows, half = into.shape
    narrow = index_ref[0]
    copies = start_blocks(narrow, whole, other, into, side, sems)
    block = pl.multiple_of((rows - 16) * (1 - narrow), 16)
    fetch = pltpu.make_async_copy(other.at[:, :, pl.ds(block, 16), :], last_ref, last_sem)
    fetch.start()
    for b, pair in enumerate(copies):
        for copy in pair:
            copy.wait()
        span = slice(16 * b, 16 * b + 16)
        for z in range(2):
            out_ref[span, z, :, :half] = jnp.swapaxes(into[:, z, span, :], 0, 1)
            out_ref[span, z, :, half:] = jnp.swapaxes(side[:, z, span, :], 0, 1)
        pltpu.make_async_copy(out_ref.at[span], out_hbm.at[span], out_sems.at[b]).start()
    fetch.wait()
    for z in range(slices):
        spot = slice(channels * z, channels * (z + 1))
        sent_ref[0, spot] = out_ref[(rows - 1) * (1 - narrow), z, :, :half]
        turned = jnp.swapaxes(last_ref[:, z], 0, 1)
        sent_ref[1, spot] = jnp.where(
            narrow == 0, turned[15].astype(f32), turned[0].astype(f32)
        ).astype(bf16)
    for b in range(rows // 16):
        span = slice(16 * b, 16 * b + 16)
        pltpu.make_async_copy(out_ref.at[span], out_hbm.at[span], out_sems.at[b]).wait()


def start_blocks(narrow, whole, other, into, side, sems):
    tile = pl.ds(pl.multiple_of(128 * narrow, 128), 128)
    copies = []
    for b in range(into.shape[2] // 16):
        span = pl.ds(16 * b, 16)
        copies.append(
            (
                pltpu.make_async_copy(whole.at[:, :, span, :], into.at[:, :, span, :], sems.at[b, 0]),
                pltpu.make_async_copy(
                    other.at[:, :, span, tile], side.at[:, :, span, :], sems.at[b, 1]
                ),
            )
        )
    for pair in copies:
        for copy in pair:
            copy.start()
    return copies


def turn_mid(index, value, other):
    channels, slices, rows, half = value.shape
    shape = (rows, slices, channels, half + 128)
    anywhere = pl.BlockSpec(memory_space=pl.ANY)
    return pl.pallas_call(
        turn_mid_kernel,
        out_shape=(pltpu.HBM(shape, bf16), jax.ShapeDtypeStruct((2, 128, half), bf16)),
        in_specs=[pl.BlockSpec(memory_space=pltpu.SMEM), anywhere, anywhere],
        out_specs=(anywhere, pl.BlockSpec(memory_space=pltpu.VMEM)),
        scratch_shapes=[
            pltpu.VMEM(value.shape, bf16),
            pltpu.VMEM((channels, slices, rows, 128), bf16),
            pltpu.SemaphoreType.DMA((rows // 16, 2)),
            pltpu.VMEM((channels, slices, 16, half), bf16),
            pltpu.SemaphoreType.DMA,
            pltpu.VMEM(shape, bf16),
            pltpu.SemaphoreType.DMA((rows // 16,)),
        ],
        compiler_params=pltpu.CompilerParams(vmem_limit_bytes=32 << 20),
        cost_estimate=pl.CostEstimate(flops=0, bytes_accessed=12 * value.size, transcendentals=0),
        name="turn_mid",
    )(index, off_chip(value), off_chip(other))


def masked_kernel(
    scale,
    index_ref,
    own_ref,
    other_ref,
    table_ref,
    table_side_ref,
    taps_ref,
    beyond_ref,
    beside_ref,
    pick_hbm,
    in_hbm,
    in_other_hbm,
    mid_hbm,
    masked_hbm,
    out_ref,
    pay_ref,
    noise_ref,
    sum_ref,
    second_ref,
    in_ref,
    in_side_ref,
    in_rows_a,
    in_rows_b,
    mid_ref,
    masked_ref,
    pick_ref,
    in_sems,
    mid_sems,
    masked_sem,
    pick_sem,
):
    wide, held, lanes = own_ref.shape
    rows = held - 8
    blocks = rows // 16
    half = mid_ref.shape[3] - 128
    ext = half + 128
    narrow = index_ref[0]
    copies = []
    for b in range(blocks):
        span = slice(16 * b, 16 * b + 16)
        copies.append(pltpu.make_async_copy(mid_hbm.at[span], mid_ref.at[span], mid_sems.at[b]))
        copies[b].start()
    channels = in_ref.shape[0]
    in_copies = start_blocks(narrow, in_hbm, in_other_hbm, in_ref, in_side_ref, in_sems)

    pick_copy = pltpu.make_async_copy(pick_hbm, pick_ref, pick_sem)
    pick_copy.start()

    lane = lanes_of((1, lanes))
    sign = jnp.where(narrow == 0, 1.0, (1 - 2 * (lane % 2)).astype(f32))
    first = (lane // 32) % 2 == 0
    z_lines = ([], [])
    for w in range(wide):
        own = own_ref[w].astype(f32) * sign
        other = other_ref[w].astype(f32) * sign
        even = jnp.where(narrow == 0, own, other)
        odd = jnp.where(narrow == 0, other, own)
        z_lines[0].append(jnp.where(first, even, pltpu.roll(odd, 32, 1)))
        z_lines[1].append(jnp.where(first, pltpu.roll(even, 96, 1), odd))
    lines = jnp.concatenate(
        [jnp.concatenate(z_lines[0], axis=1), jnp.concatenate(z_lines[1], axis=1)], axis=0
    )
    lines = lines.astype(bf16)
    noise = jnp.concatenate(
        [
            dot_nt(lines, table[0]) + dot_nt(lines, table[1])
            for table in (table_ref, table_side_ref)
        ],
        axis=1,
    )
    column = lanes_of((1, ext))
    beside = jnp.where(narrow == 0, column - half, ext - 1 - column) < 2
    ours = (column < half) | beside
    noise = jnp.where(ours, noise * scale, 0.0).astype(bf16).astype(f32)
    for d in range(3):
        moved = noise if d == 1 else pltpu.roll(noise, (d - 1) % ext, 1)
        for z in range(2):
            noise_ref[d, z] = moved[z * held : (z + 1) * held]

    side_lane = jnp.where(narrow == 0, half, ext - 1)
    kept = (column < half) | (column == side_lane)

    def window_of(start):
        pieces = [noise_ref[d, z, start : start + 16, :] for z in range(2) for d in range(3)]
        return jnp.concatenate(pieces + [jnp.zeros((32, ext), f32)], axis=0).astype(bf16)

    def store_rows(window, tap_row, mask, row, count):
        value = dot(taps_ref[tap_row * 128 : (tap_row + count) * 128, :], window)
        value = jnp.where(mask.astype(f32) > 0, jnp.where(kept, value, 0.0), 0.0)
        masked_ref[row * 128 : (row + count) * 128, :] = value.astype(bf16)

    for b in range(blocks):
        copies[b].wait()
        for h in range(2):
            window = window_of(16 * b + 8 * h)
            mid = mid_ref[16 * b + 8 * h : 16 * b + 8 * h + 8].reshape(1024, ext)
            second = dot_nt(mid[:, :half], window[:, :half])
            second_ref[...] = second if b == 0 and h == 0 else second_ref[...] + second
            for m in range(0, 8, 2):
                store_rows(
                    window, m + 1, mid[m * 128 : m * 128 + 256], 16 * b + 8 * h + m + 1, 2
                )
    for k in range(2):
        main = jnp.where(narrow == k, beyond_ref[0].astype(f32), beside_ref[1].astype(f32))
        aside = jnp.where(narrow == k, beyond_ref[1].astype(f32), beside_ref[0].astype(f32))
        aside = jnp.where(narrow == 0, aside[:, :128], aside[:, half - 128 :])
        mask = jnp.concatenate([main, aside], axis=1)
        store_rows(window_of((rows - 8) * k), 9 * k, mask, (rows + 1) * k, 1)
    keep = pltpu.make_async_copy(masked_ref, masked_hbm, masked_sem)
    keep.start()

    amount = jnp.where(narrow == 0, 127, 1)

    def turn_in(b, into):
        for copy in in_copies[b]:
            copy.wait()
        span = slice(16 * b, 16 * b + 16)
        for z in range(2):
            turned = jnp.swapaxes(in_ref[:, z, span, :], 0, 1)
            into[1, :, z] = turned
            flat = turned.reshape(16 * channels, half).astype(f32)
            beside = jnp.swapaxes(in_side_ref[:, z, span, :], 0, 1)
            beside = pltpu.roll(beside.reshape(16 * channels, 128).astype(f32), amount, 1)
            left = flat[:, :128]
            right = flat[:, 128:]
            down_left = pltpu.roll(left, 1, 1)
            down_right = pltpu.roll(right, 1, 1)
            up_left = pltpu.roll(left, 127, 1)
            up_right = pltpu.roll(right, 127, 1)
            from_before = jnp.where(narrow == 0, 0.0, beside)
            from_after = jnp.where(narrow == 0, beside, 0.0)
            moved = {
                (0, 0): jnp.where(lane == 0, from_before, down_left),
                (0, 1): jnp.where(lane == 0, down_left, down_right),
                (2, 0): jnp.where(lane == 127, up_right, up_left),
                (2, 1): jnp.where(lane == 127, from_after, up_right),
            }
            for (d, t), value in moved.items():
                into[d, :, z, :, 128 * t : 128 * t + 128] = value.astype(bf16).reshape(
                    16, channels, 128
                )

    in_rows = (in_rows_a, in_rows_b)
    turn_in(0, in_rows[0])
    for b in range(blocks):
        if b + 1 < blocks:
            turn_in(b + 1, in_rows[(b + 1) % 2])
        held_rows = in_rows[b % 2]
        left = jnp.concatenate(
            [
                masked_ref[(16 * b + 2 * q) * 128 : (16 * b + 2 * q + 4) * 128, :half]
                for q in range(8)
            ],
            axis=1,
        )
        for d in range(3):
            right = jnp.concatenate(
                [held_rows[d, 2 * q : 2 * q + 2].reshape(256, half) for q in range(8)], axis=1
            )
            part = dot_nt(left, right)
            sum_ref[d] = part if b == 0 else sum_ref[d] + part

    singles = []
    for d in range(3):
        for dx in range(3):
            total = None
            for par in range(2):
                i4 = par + 2 - dx
                block = sum_ref[d, i4 * 128 : (i4 + 1) * 128, par * 128 : (par + 1) * 128]
                total = block if total is None else total + block
            turned = total.T
            upper = turned[:64]
            lower = turned[64:]
            slot = d * 3 + dx
            pay_ref[slot * 64 : (slot + 1) * 64] = jnp.where(lane < 64, lower, upper)
            singles.append(upper + pltpu.roll(lower, 64, 1))
    pieces = [
        second_ref[(m * 2 + z) * 64 : (m * 2 + z + 1) * 64, :] for m in range(8) for z in range(2)
    ]
    pick_copy.wait()
    second = jnp.dot(
        jnp.concatenate(pieces, axis=1), pick_ref[...].astype(f32), preferred_element_type=f32, precision=highest
    )
    singles.append(second)
    for k in range(5):
        pay_ref[(9 + k) * 64 : (10 + k) * 64] = jnp.where(
            lane < 64, singles[2 * k], pltpu.roll(singles[2 * k + 1], 64, 1)
        )
    out_ref[...] = pay_ref[...].astype(bf16)
    keep.wait()


def masked_and_kernels(
    index,
    own,
    other,
    table,
    table_side,
    taps,
    pick,
    beyond,
    beyond_other,
    act_in,
    in_other,
    rows_mid,
    scale,
):
    wide, held, lanes = own.shape
    rows, slices, channels, ext = rows_mid.shape
    vmem = pl.BlockSpec(memory_space=pltpu.VMEM)
    anywhere = pl.BlockSpec(memory_space=pl.ANY)
    return pl.pallas_call(
        functools.partial(masked_kernel, scale),
        out_shape=(
            pltpu.HBM(((rows + 2) * 128, ext), bf16),
            jax.ShapeDtypeStruct((14 * 64, 128), bf16),
        ),
        in_specs=[pl.BlockSpec(memory_space=pltpu.SMEM)] + [vmem] * 7 + [anywhere] * 4,
        out_specs=(anywhere, vmem),
        scratch_shapes=[
            pltpu.VMEM((14 * 64, 128), f32),
            pltpu.VMEM((3, 2, held, ext), f32),
            pltpu.VMEM((3, 512, 256), f32),
            pltpu.VMEM((1024, 128), f32),
            pltpu.VMEM(act_in.shape, bf16),
            pltpu.VMEM((channels, slices, rows, 128), bf16),
            pltpu.VMEM((3, 16, slices, channels, ext - 128), bf16),
            pltpu.VMEM((3, 16, slices, channels, ext - 128), bf16),
            pltpu.VMEM(rows_mid.shape, bf16),
            pltpu.VMEM(((rows + 2) * 128, ext), bf16),
            pltpu.VMEM(pick.shape, bf16),
            pltpu.SemaphoreType.DMA((rows // 16, 2)),
            pltpu.SemaphoreType.DMA((rows // 16,)),
            pltpu.SemaphoreType.DMA,
            pltpu.SemaphoreType.DMA,
        ],
        compiler_params=pltpu.CompilerParams(vmem_limit_bytes=48 << 20),
        name="masked_and_kernels",
    )(
        index,
        own,
        other,
        off_chip(table),
        off_chip(table_side),
        taps,
        beyond,
        beyond_other,
        off_chip(pick),
        off_chip(act_in),
        off_chip(in_other),
        off_chip(rows_mid),
    )


def arrange_kernel(taps_ref, weight_ref):
    for dy in range(3):
        for par, i4 in ((0, 3), (1, 0)):
            weight_ref[
                par * 128 : (par + 1) * 128, dy * 512 + i4 * 128 : dy * 512 + (i4 + 1) * 128
            ] = jnp.zeros((128, 128), bf16)
        for dx in range(3):
            for z in range(2):
                tap = dx * 3 + dy
                tile = jnp.concatenate([taps_ref[(z + 1) * 9 + tap], taps_ref[z * 9 + tap]], axis=1)
                for par in range(2):
                    spot = dy * 512 + (par + 2 - dx) * 128
                    weight_ref[
                        par * 128 + z * 64 : par * 128 + (z + 1) * 64, spot : spot + 128
                    ] = tile


def arrange(w_first):
    vmem = pl.BlockSpec(memory_space=pltpu.VMEM)
    return pl.pallas_call(
        arrange_kernel,
        out_shape=jax.ShapeDtypeStruct((256, 1536), bf16),
        in_specs=[vmem],
        out_specs=vmem,
        name="arrange",
    )(w_first)


def input_kernel(base, masked_hbm, weight_ref, *rest):
    out_hbm, masked_ref, shifted_ref, wide_ref, out_ref, in_sems, out_sems = rest[-7:]
    rows = shifted_ref.shape[1] // 128 - 2
    fetches = []
    for step in range(rows // 8):
        first = 0 if step == 0 else (8 * step + 2) * 128
        last = (8 * step + 10) * 128
        fetches.append(
            pltpu.make_async_copy(
                masked_hbm.at[base * 128 + first : base * 128 + last],
                masked_ref.at[first:last],
                in_sems.at[step],
            )
        )
        fetches[step].start()
    ext = masked_ref.shape[1]
    half = ext - 128
    channels = out_ref.shape[1]
    def shift(row):
        spot = slice(row * 128, (row + 1) * 128)
        whole = masked_ref[spot, :]
        shifted_ref[1, spot, :] = whole[:, :half]
        whole = whole.astype(f32)
        for d in (0, 2):
            shifted_ref[d, spot, :] = pltpu.roll(whole, (d - 1) % ext, 1)[:, :half].astype(bf16)

    ready = 0
    outs = []
    for step in range(rows // 8):
        fetches[step].wait()
        while ready < 8 * step + 10:
            shift(ready)
            ready += 1
        for q in range(4):
            row = (8 * step + 2 * q) * 128
            stacked = jnp.concatenate(
                [shifted_ref[d, row : row + 512, :] for d in range(3)], axis=0
            )
            value = dot(weight_ref[...], stacked).astype(bf16)
            wide_ref[step % 4, 2 * q * 128 : (2 * q + 2) * 128, :] = value
        if step % 2 == 1:
            block = step // 2
            pair = jnp.concatenate([wide_ref[(step - 1) % 4], wide_ref[step % 4]], axis=0)
            pair = pair.reshape(16, 2, channels, half)
            for z in range(2):
                out_ref[block, :, z] = jnp.swapaxes(pair[:, z], 0, 1)
            first = base + 16 * block
            copy = pltpu.make_async_copy(
                out_ref.at[block], out_hbm.at[:, :, first : first + 16, :], out_sems.at[block]
            )
            copy.start()
            outs.append(copy)
    for copy in outs:
        copy.wait()


def input_gradient(masked, weight, base, rows, shape, earlier=None):
    ext = masked.shape[1]
    half = ext - 128
    channels = shape[0]
    anywhere = pl.BlockSpec(memory_space=pl.ANY)
    extra = () if earlier is None else (earlier,)
    return pl.pallas_call(
        functools.partial(input_kernel, base),
        out_shape=jax.ShapeDtypeStruct(shape, bf16),
        in_specs=[anywhere, pl.BlockSpec(memory_space=pltpu.VMEM)] + [anywhere] * len(extra),
        out_specs=anywhere,
        scratch_shapes=[
            pltpu.VMEM(((rows + 2) * 128, ext), bf16),
            pltpu.VMEM((3, (rows + 2) * 128, half), bf16),
            pltpu.VMEM((4, 1024, half), bf16),
            pltpu.VMEM((rows // 16, channels, 2, 16, half), bf16),
            pltpu.SemaphoreType.DMA((rows // 8,)),
            pltpu.SemaphoreType.DMA((rows // 16,)),
        ],
        input_output_aliases={} if earlier is None else {2: 0},
        cost_estimate=pl.CostEstimate(
            flops=2 * rows * 128 * half * 1536, bytes_accessed=4 * rows * 128 * half * 2, transcendentals=0
        ),
        compiler_params=pltpu.CompilerParams(vmem_limit_bytes=30 << 20),
        name="input_gradient",
    )(off_chip(masked), weight, *extra)


def unpack_kernel(pay_ref, first_ref, second_ref):
    slots = [pay_ref[64 * k : 64 * k + 64].astype(f32) for k in range(14)]
    for slot in range(9):
        tap = slot % 3 * 3 + slot // 3
        first_ref[18 + tap] = slots[slot][:, :64]
        first_ref[tap] = pltpu.roll(slots[slot], 64, 1)[:, :64]
        single = slots[9 + slot // 2]
        if slot % 2 == 1:
            single = pltpu.roll(single, 64, 1)
        first_ref[9 + tap] = single[:, :64]
    second_ref[...] = pltpu.roll(slots[13], 64, 1).T[:27]


def unpack(pay):
    vmem = pl.BlockSpec(memory_space=pltpu.VMEM)
    return pl.pallas_call(
        unpack_kernel,
        out_shape=(
            jax.ShapeDtypeStruct((27, 64, 64), f32),
            jax.ShapeDtypeStruct((27, 64), f32),
        ),
        in_specs=[vmem],
        out_specs=(vmem, vmem),
        name="unpack",
    )(on_chip(pay))


def tap_choice():
    choice = np.zeros((27, 10, 2, 128), np.float32)
    for dz in (-1, 0, 1):
        for dx in (-1, 0, 1):
            for dy in (-1, 0, 1):
                tap = (dz + 1) * 9 + (dx + 1) * 3 + dy + 1
                for m in range(-1, 9):
                    for z in range(2):
                        if 0 <= z - dz < 2:
                            r = m + 2 - dx
                            choice[tap, m + 1, z, ((z - dz) * 3 + dy + 1) * 16 + r] = 1
    return choice


def fast(denoised, clean_volume, weight, act_in, act_mid, w_first, w_second):
    wide = lax.axis_size("wide")
    slices, rows, half = denoised.shape
    channels = act_in.shape[0]
    keep = weight.shape[0]
    total_x = wide * rows
    total_y = 2 * half
    ext = half + 128
    narrow = lax.axis_index("narrow")
    index = narrow.astype(jnp.int32).reshape(1)
    swap = [(0, 1), (1, 0)]
    up = [(i, i + 1) for i in range(wide - 1)]
    down = [(j, i) for i, j in up]
    table_y, table_side = (jnp.asarray(t) for t in y_table(wide, keep, half))
    table_x = jnp.asarray(x_table(total_x))
    choice = tap_choice()
    pick = np.zeros((16 * 128, 128), np.float32)
    pick[:, :27] = choice[:, 1:9].reshape(27, 16 * 128).T

    error = denoised - clean_volume
    error_other = lax.ppermute(error, "narrow", swap)
    act_mid, act_in, error_other = lax.optimization_barrier((act_mid, act_in, error_other))
    mid_other = lax.ppermute(act_mid, "narrow", swap)
    in_other = lax.ppermute(act_in, "narrow", swap)
    lines = forward_y(index, error, error_other, table_y, wide)

    lines, act_mid, weight = lax.optimization_barrier((lines, act_mid, weight))
    lines = lax.all_to_all(lines, "wide", 0, 0, tiled=True)
    rows_mid, sent = turn_mid(index, act_mid, mid_other)
    ways = [(2 * i, 2 * j) for i, j in up] + [(2 * i + 1, 2 * j + 1) for i, j in down]
    beyond = lax.ppermute(sent, ("wide", "narrow"), ways)
    weight_lines = jnp.tile(weight.T, (1, 4))
    lines, weight_lines = lax.optimization_barrier((lines, weight_lines))
    lines = along_x(lines, table_x, weight_lines)

    lines, beyond, w_first, w_second = lax.optimization_barrier((lines, beyond, w_first, w_second))
    lines = lax.all_to_all(lines, "wide", 0, 0, tiled=True)
    beyond_other = lax.ppermute(beyond, "narrow", swap)
    matrix = arrange(w_first)
    taps = jnp.einsum(
        "tc,tmzk->mzck", w_second, jnp.asarray(choice, bf16), preferred_element_type=f32
    )
    taps = taps.astype(bf16).reshape(1280, 128)
    lines, matrix, taps, beyond_other = lax.optimization_barrier(
        (lines, matrix, taps, beyond_other)
    )
    lines_other = lax.ppermute(lines, "narrow", swap)
    masked, pay = masked_and_kernels(
        index,
        lines,
        lines_other,
        table_y,
        table_side,
        taps,
        jnp.asarray(pick, bf16),
        beyond,
        beyond_other,
        act_in,
        in_other,
        rows_mid,
        -2.0 / (total_x * total_y),
    )

    pay = pay.reshape(wide, pay.shape[0] // wide, 128)
    pay, matrix = lax.optimization_barrier((pay, matrix))
    pay = lax.all_to_all(pay, "wide", 0, 0, tiled=True)
    grad_in = input_gradient(masked, matrix, 0, rows // 2, act_in.shape)
    pay, grad_in = lax.optimization_barrier((pay, grad_in))
    total = pay.astype(f32).sum(axis=0)
    total = total + lax.ppermute(total, "narrow", swap)
    pay = jnp.broadcast_to(total.astype(bf16)[None], pay.shape)
    pay, grad_in, matrix = lax.optimization_barrier((pay, grad_in, matrix))
    pay = lax.all_to_all(pay, "wide", 0, 0, tiled=True)
    grad_in = input_gradient(masked, matrix, rows // 2, rows // 2, act_in.shape, grad_in)
    pay, grad_in = lax.optimization_barrier((pay, grad_in))
    grad_first, grad_second = unpack(pay.reshape(-1, 128))
    return (grad_in, grad_first, grad_second)


def with_halo(x, sides, width):
    for axis, dim in sides:
        devices, length = (lax.axis_size(axis), x.shape[dim])
        up = [(i, (i + 1) % devices) for i in range(devices - 1)]
        down = [(j, i) for i, j in up]
        last = lax.slice_in_dim(x, length - width, length, axis=dim)
        first = lax.slice_in_dim(x, 0, width, axis=dim)
        before = lax.ppermute(last, axis, up)
        after = lax.ppermute(first, axis, down)
        x = jnp.concatenate([before, x, after], axis=dim)
    return x


def phase_table(left_index, right_index, length):
    product = left_index[:, None] * right_index[None, :] % length
    angles = product.astype(jnp.float32) * (two_pi / length)
    return (jnp.cos(angles), jnp.sin(angles))


def shifted_windows(padded, slices, rows_x, cols_y, taps_list):
    windows = []
    for tap_index in taps_list:
        step_z = tap_index // 9 - 1
        step_x = tap_index // 3 % 3 - 1
        step_y = tap_index % 3 - 1
        windows.append(
            padded[
                ...,
                1 - step_z : 1 - step_z + slices,
                1 - step_x : 1 - step_x + rows_x,
                1 - step_y : 1 - step_y + cols_y,
            ]
        )
    return jnp.stack(windows, axis=0)


def plain(denoised, clean_volume, weight, act_in, act_mid, w_first, w_second):
    wide_count = lax.axis_size("wide")
    narrow_count = lax.axis_size("narrow")
    slices, rows_x, half_cols = denoised.shape
    total_y = half_cols * narrow_count
    total_x = rows_x * wide_count
    kept_cols = half_cols // wide_count
    narrow_index = lax.axis_index("narrow")
    error_field = denoised - clean_volume
    columns = lax.iota(jnp.int32, total_y)
    frequency = (
        columns % half_cols // kept_cols * narrow_count + columns // half_cols
    ) * kept_cols + columns % kept_cols
    own_rows = narrow_index * half_cols + lax.iota(jnp.int32, half_cols)
    cos_y, sin_y = phase_table(own_rows, frequency, total_y)
    part_real = jnp.einsum("zxy,yc->zxc", error_field, cos_y, precision=highest)
    part_imag = -jnp.einsum("zxy,yc->zxc", error_field, sin_y, precision=highest)
    spec_real, spec_imag = (
        lax.psum_scatter(part_real, "narrow", scatter_dimension=2, tiled=True),
        lax.psum_scatter(part_imag, "narrow", scatter_dimension=2, tiled=True),
    )
    positions = lax.iota(jnp.int32, total_x)
    cos_x, sin_x = phase_table(positions, positions, total_x)
    pieces = (
        lax.all_to_all(
            spec_real.reshape(slices, rows_x, wide_count, kept_cols),
            "wide",
            split_axis=2,
            concat_axis=1,
            tiled=True,
        ),
        lax.all_to_all(
            spec_imag.reshape(slices, rows_x, wide_count, kept_cols),
            "wide",
            split_axis=2,
            concat_axis=1,
            tiled=True,
        ),
    )
    item_count = pieces[0].shape[0]
    in_real = pieces[0].reshape(item_count, total_x, kept_cols)
    in_imag = pieces[1].reshape(item_count, total_x, kept_cols)
    four_real = jnp.einsum("mxk,xq->mkq", in_real, cos_x, precision=highest) + jnp.einsum(
        "mxk,xq->mkq", in_imag, sin_x, precision=highest
    )
    four_imag = jnp.einsum("mxk,xq->mkq", in_imag, cos_x, precision=highest) - jnp.einsum(
        "mxk,xq->mkq", in_real, sin_x, precision=highest
    )
    weighted_real = weight * four_real
    weighted_imag = weight * four_imag
    out_real = jnp.einsum("mkq,qx->mxk", weighted_real, cos_x, precision=highest) - jnp.einsum(
        "mkq,qx->mxk", weighted_imag, sin_x, precision=highest
    )
    out_imag = jnp.einsum("mkq,qx->mxk", weighted_imag, cos_x, precision=highest) + jnp.einsum(
        "mkq,qx->mxk", weighted_real, sin_x, precision=highest
    )
    back_real = lax.all_to_all(
        out_real.reshape(item_count, wide_count, rows_x, kept_cols),
        "wide",
        split_axis=1,
        concat_axis=3,
        tiled=True,
    ).reshape(item_count, rows_x, half_cols)
    back_imag = lax.all_to_all(
        out_imag.reshape(item_count, wide_count, rows_x, kept_cols),
        "wide",
        split_axis=1,
        concat_axis=3,
        tiled=True,
    ).reshape(item_count, rows_x, half_cols)
    local_cols = lax.iota(jnp.int32, half_cols)
    own_freq = (
        local_cols // kept_cols * narrow_count + narrow_index
    ) * kept_cols + local_cols % kept_cols
    cos_back, sin_back = phase_table(own_freq, columns, total_y)
    part_term = jnp.einsum("zxc,cy->zxy", back_real, cos_back, precision=highest) - jnp.einsum(
        "zxc,cy->zxy", back_imag, sin_back, precision=highest
    )
    field_real = lax.psum_scatter(part_term, "narrow", scatter_dimension=2, tiled=True)
    grad_noise = (field_real * (-2.0 / (total_x * total_y))).astype(jnp.bfloat16)
    noise_rim = with_halo(grad_noise, (("wide", 1), ("narrow", 2)), 1)
    noise_pad = jnp.pad(noise_rim, ((1, 1), (0, 0), (0, 0)))
    noise_windows = shifted_windows(noise_pad, slices, rows_x, half_cols, range(27))
    grad_mid = jnp.einsum(
        "tc,tzxy->czxy", w_second, noise_windows, preferred_element_type=jnp.float32
    )
    masked = jnp.where(act_mid > 0, grad_mid, 0.0).astype(jnp.bfloat16)
    masked_rim = with_halo(masked, (("wide", 2), ("narrow", 3)), 1)
    grad_second = jnp.einsum(
        "czxy,tzxy->tc", act_mid, noise_windows, preferred_element_type=jnp.float32
    )
    masked_pad = jnp.pad(masked_rim, ((0, 0), (1, 1), (0, 0), (0, 0)))
    channels = act_in.shape[0]
    grad_in = jnp.zeros(act_in.shape, jnp.float32)
    first_parts = []
    for plane_index in range(9):
        stacked = shifted_windows(
            masked_pad, slices, rows_x, half_cols, [plane_index, plane_index + 9, plane_index + 18]
        )
        first_parts.append(
            jnp.einsum("izxy,dozxy->dio", act_in, stacked, preferred_element_type=jnp.float32)
        )
        grad_in = grad_in + jnp.einsum(
            "dio,dozxy->izxy", w_first[plane_index::9], stacked, preferred_element_type=jnp.float32
        )
    grad_first = jnp.stack(first_parts, axis=1).reshape(27, channels, channels)
    grad_first, grad_second = lax.psum((grad_first, grad_second), ("wide", "narrow"))
    return (grad_in.astype(jnp.bfloat16), grad_first, grad_second)


def shards(denoised, clean_volume, weight, act_in, act_mid, w_first, w_second):
    sizes = (
        lax.axis_size("wide"),
        lax.axis_size("narrow"),
        *denoised.shape,
        weight.shape[0],
        act_in.shape[0],
    )
    chosen = fast if sizes == (8, 2, 2, 64, 256, 32, 64) else plain
    return chosen(denoised, clean_volume, weight, act_in, act_mid, w_first, w_second)


def solution(mesh):
    placed = (
        P("grp", "wide", "narrow"),
        P("grp", "wide", "narrow"),
        P(("wide", "narrow"), None),
        P(None, "grp", "wide", "narrow"),
        P(None, "grp", "wide", "narrow"),
        P(),
        P(),
    )
    return jax.shard_map(
        shards,
        mesh=mesh,
        in_specs=placed,
        out_specs=(P(None, "grp", "wide", "narrow"), P("grp", None, None), P("grp", None)),
        check_vma=False,
    )
```

```python
import functools

import jax
import jax.numpy as jnp
import ml_dtypes
import numpy as np
from jax import lax
from jax.experimental import pallas as pl
from jax.experimental.pallas import tpu as pltpu
from jax.sharding import PartitionSpec as P

two_pi = 6.283185307179586
highest = lax.Precision.HIGHEST
bf16 = jnp.bfloat16
f32 = jnp.float32


def split_table(table):
    high = table.astype(np.float32).astype(ml_dtypes.bfloat16)
    low = (table - high.astype(np.float64)).astype(np.float32).astype(ml_dtypes.bfloat16)
    return np.stack([high, low])


def cos_sin(left, right, length):
    angles = (np.outer(left, right) % length) * (2.0 * np.pi / length)
    return np.cos(angles), np.sin(angles)


def y_table(wide, keep, half):
    total = 2 * half
    ky = np.arange(total)
    rows = np.zeros(half + 128, np.int64)
    used = np.zeros(half + 128)
    rows[:half] = np.arange(half)
    used[:half] = 1
    for lane, y in ((0, half), (1, half + 1), (127, -1), (126, -2)):
        rows[half + lane] = y
        used[half + lane] = 1
    cos, sin = cos_sin(rows, ky, total)
    cos, sin = cos * used[:, None], -sin * used[:, None]
    shape = (half + 128, wide, 2, keep)
    both = np.stack([cos.reshape(shape), sin.reshape(shape)], axis=2)
    table = split_table(both.reshape(half + 128, wide * 4 * keep))
    return table[:, :half], table.transpose(0, 2, 1).copy()


def x_table(total):
    index = np.arange(total)
    cos, sin = cos_sin(index, index, total)
    return split_table(np.concatenate([cos, sin], axis=0))


def dot(a, b):
    return jnp.dot(a, b, preferred_element_type=f32)


def dot_nt(a, b):
    return lax.dot_general(a, b, (((1,), (1,)), ((), ())), preferred_element_type=f32)


def parts_of(x):
    high = x.astype(bf16)
    return high, (x - high.astype(f32)).astype(bf16)


def lanes_of(shape):
    return lax.broadcasted_iota(jnp.int32, shape, len(shape) - 1)


def on_chip(x):
    return pltpu.with_memory_space_constraint(x, pltpu.VMEM)


def off_chip(x):
    return pltpu.with_memory_space_constraint(x, pltpu.HBM)


def forward_y_kernel(index_ref, own_ref, other_ref, table_ref, out_ref):
    slices, rows, half = own_ref.shape
    wide = out_ref.shape[0]
    narrow = index_ref[0]
    stacked = jnp.concatenate(
        [own_ref[...].reshape(slices * rows, half), other_ref[...].reshape(slices * rows, half)],
        axis=0,
    )
    high, low = parts_of(stacked)
    t_high = table_ref[0]
    t_low = table_ref[1]
    total = dot(high, t_high) + dot(low, t_high) + dot(high, t_low)
    lane = lanes_of((1, 128))
    sign = (1 - 2 * (lane % 2)).astype(f32)
    own_scale = jnp.where(narrow == 0, 1.0, sign)
    other_scale = jnp.where(narrow == 0, sign, 1.0)
    first = (lane // 32) % 2 == 0
    count = slices * rows
    for w in range(wide):
        cols = slice(128 * w, 128 * (w + 1))
        merged = total[:count, cols] * own_scale + total[count:, cols] * other_scale
        z0 = merged[:rows]
        z1 = merged[rows:]
        as_zero = jnp.where(first, z0, pltpu.roll(z1, 32, 1))
        as_one = jnp.where(first, pltpu.roll(z0, 96, 1), z1)
        out_ref[w] = jnp.where(narrow == 0, as_zero, as_one)


def forward_y(index, own, other, table, wide):
    slices, rows, half = own.shape
    return pl.pallas_call(
        forward_y_kernel,
        out_shape=jax.ShapeDtypeStruct((wide, rows, 128), f32),
        in_specs=[pl.BlockSpec(memory_space=pltpu.SMEM)] + [pl.BlockSpec(memory_space=pltpu.VMEM)] * 3,
        out_specs=pl.BlockSpec(memory_space=pltpu.VMEM),
        compiler_params=pltpu.CompilerParams(vmem_limit_bytes=10 << 20),
        name="forward_y",
    )(index, own, other, off_chip(table))


def along_x_kernel(in_ref, table_ref, weight_ref, out_ref, line_ref):
    wide, rows, lanes = in_ref.shape
    total = wide * rows
    held = out_ref.shape[1]
    lane = lanes_of((1, lanes))
    sign = jnp.where(lane < 64, 1.0, -1.0)
    t_high = table_ref[0]
    t_low = table_ref[1]

    def transform(value):
        high, low = parts_of(value)
        both = dot(t_high, jnp.concatenate([high, low], axis=1))
        return both[:, :lanes] + both[:, lanes:] + dot(t_low, high)

    spread = transform(in_ref[...].reshape(total, lanes))
    spectrum = spread[:total] + sign * pltpu.roll(spread[total:], 64, 1)
    back = transform(spectrum * weight_ref[...])
    line_ref[:8] = jnp.zeros((8, lanes), f32)
    line_ref[8 + total :] = jnp.zeros((8, lanes), f32)
    line_ref[8 : 8 + total] = back[:total] - sign * pltpu.roll(back[total:], 64, 1)
    for w in range(wide):
        out_ref[w] = line_ref[6 + rows * w : 6 + rows * w + held].astype(out_ref.dtype)


def along_x(pieces, table, weight_lines):
    wide, rows, lanes = pieces.shape
    return pl.pallas_call(
        along_x_kernel,
        out_shape=jax.ShapeDtypeStruct((wide, rows + 8, lanes), bf16),
        in_specs=[pl.BlockSpec(memory_space=pltpu.VMEM)] * 3,
        out_specs=pl.BlockSpec(memory_space=pltpu.VMEM),
        scratch_shapes=[pltpu.VMEM((wide * rows + 16, lanes), f32)],
        compiler_params=pltpu.CompilerParams(vmem_limit_bytes=12 << 20),
        name="along_x",
    )(pieces, table, weight_lines)


def turn_mid_kernel(
    index_ref, whole, other, out_hbm, sent_ref, into, side, sems, last_ref, last_sem, out_ref, out_sems
):
    channels, slices, rows, half = into.shape
    narrow = index_ref[0]
    copies = start_blocks(narrow, whole, other, into, side, sems)
    block = pl.multiple_of((rows - 16) * (1 - narrow), 16)
    fetch = pltpu.make_async_copy(other.at[:, :, pl.ds(block, 16), :], last_ref, last_sem)
    fetch.start()
    for b, pair in enumerate(copies):
        for copy in pair:
            copy.wait()
        span = slice(16 * b, 16 * b + 16)
        for z in range(2):
            out_ref[span, z, :, :half] = jnp.swapaxes(into[:, z, span, :], 0, 1)
            out_ref[span, z, :, half:] = jnp.swapaxes(side[:, z, span, :], 0, 1)
        pltpu.make_async_copy(out_ref.at[span], out_hbm.at[span], out_sems.at[b]).start()
    fetch.wait()
    for z in range(slices):
        spot = slice(channels * z, channels * (z + 1))
        sent_ref[0, spot] = out_ref[(rows - 1) * (1 - narrow), z, :, :half]
        turned = jnp.swapaxes(last_ref[:, z], 0, 1)
        sent_ref[1, spot] = jnp.where(
            narrow == 0, turned[15].astype(f32), turned[0].astype(f32)
        ).astype(bf16)
    for b in range(rows // 16):
        span = slice(16 * b, 16 * b + 16)
        pltpu.make_async_copy(out_ref.at[span], out_hbm.at[span], out_sems.at[b]).wait()


def start_blocks(narrow, whole, other, into, side, sems):
    tile = pl.ds(pl.multiple_of(128 * narrow, 128), 128)
    copies = []
    for b in range(into.shape[2] // 16):
        span = pl.ds(16 * b, 16)
        copies.append(
            (
                pltpu.make_async_copy(whole.at[:, :, span, :], into.at[:, :, span, :], sems.at[b, 0]),
                pltpu.make_async_copy(
                    other.at[:, :, span, tile], side.at[:, :, span, :], sems.at[b, 1]
                ),
            )
        )
    for pair in copies:
        for copy in pair:
            copy.start()
    return copies


def turn_mid(index, value, other):
    channels, slices, rows, half = value.shape
    shape = (rows, slices, channels, half + 128)
    anywhere = pl.BlockSpec(memory_space=pl.ANY)
    return pl.pallas_call(
        turn_mid_kernel,
        out_shape=(pltpu.HBM(shape, bf16), jax.ShapeDtypeStruct((2, 128, half), bf16)),
        in_specs=[pl.BlockSpec(memory_space=pltpu.SMEM), anywhere, anywhere],
        out_specs=(anywhere, pl.BlockSpec(memory_space=pltpu.VMEM)),
        scratch_shapes=[
            pltpu.VMEM(value.shape, bf16),
            pltpu.VMEM((channels, slices, rows, 128), bf16),
            pltpu.SemaphoreType.DMA((rows // 16, 2)),
            pltpu.VMEM((channels, slices, 16, half), bf16),
            pltpu.SemaphoreType.DMA,
            pltpu.VMEM(shape, bf16),
            pltpu.SemaphoreType.DMA((rows // 16,)),
        ],
        compiler_params=pltpu.CompilerParams(vmem_limit_bytes=32 << 20),
        cost_estimate=pl.CostEstimate(flops=0, bytes_accessed=12 * value.size, transcendentals=0),
        name="turn_mid",
    )(index, off_chip(value), off_chip(other))


def masked_kernel(
    scale,
    index_ref,
    own_ref,
    other_ref,
    table_ref,
    taps_ref,
    beyond_ref,
    beside_ref,
    pick_hbm,
    in_hbm,
    in_other_hbm,
    mid_hbm,
    masked_hbm,
    out_ref,
    pay_ref,
    noise_ref,
    sum_ref,
    second_ref,
    in_ref,
    in_side_ref,
    in_rows_a,
    in_rows_b,
    mid_ref,
    masked_ref,
    pick_ref,
    in_sems,
    mid_sems,
    masked_sem,
    pick_sem,
):
    wide, held, lanes = own_ref.shape
    rows = held - 8
    blocks = rows // 16
    half = mid_ref.shape[3] - 128
    ext = half + 128
    narrow = index_ref[0]
    copies = []
    for b in range(blocks):
        span = slice(16 * b, 16 * b + 16)
        copies.append(pltpu.make_async_copy(mid_hbm.at[span], mid_ref.at[span], mid_sems.at[b]))
        copies[b].start()
    channels = in_ref.shape[0]
    in_copies = start_blocks(narrow, in_hbm, in_other_hbm, in_ref, in_side_ref, in_sems)

    pick_copy = pltpu.make_async_copy(pick_hbm, pick_ref, pick_sem)
    pick_copy.start()

    lane = lanes_of((1, lanes))
    sign = jnp.where(narrow == 0, 1.0, (1 - 2 * (lane % 2)).astype(f32))
    first = (lane // 32) % 2 == 0
    z_lines = ([], [])
    for w in range(wide):
        own = own_ref[w].astype(f32) * sign
        other = other_ref[w].astype(f32) * sign
        even = jnp.where(narrow == 0, own, other)
        odd = jnp.where(narrow == 0, other, own)
        z_lines[0].append(jnp.where(first, even, pltpu.roll(odd, 32, 1)))
        z_lines[1].append(jnp.where(first, pltpu.roll(even, 96, 1), odd))
    lines = jnp.concatenate(
        [jnp.concatenate(z_lines[0], axis=1), jnp.concatenate(z_lines[1], axis=1)], axis=0
    )
    lines = lines.astype(bf16)
    noise = dot(lines, table_ref[0]) + dot(lines, table_ref[1])
    column = lanes_of((1, ext))
    beside = jnp.where(narrow == 0, column - half, ext - 1 - column) < 2
    ours = (column < half) | beside
    noise = jnp.where(ours, noise * scale, 0.0).astype(bf16).astype(f32)
    for d in range(3):
        moved = noise if d == 1 else pltpu.roll(noise, (d - 1) % ext, 1)
        for z in range(2):
            noise_ref[d, z] = moved[z * held : (z + 1) * held]

    side_lane = jnp.where(narrow == 0, half, ext - 1)
    kept = (column < half) | (column == side_lane)

    def window_of(start):
        pieces = [noise_ref[d, z, start : start + 16, :] for z in range(2) for d in range(3)]
        return jnp.concatenate(pieces + [jnp.zeros((32, ext), f32)], axis=0).astype(bf16)

    def store_rows(window, tap_row, mask, row, count):
        value = dot(taps_ref[tap_row * 128 : (tap_row + count) * 128, :], window)
        value = jnp.where(mask.astype(f32) > 0, jnp.where(kept, value, 0.0), 0.0)
        masked_ref[row * 128 : (row + count) * 128, :] = value.astype(bf16)

    for b in range(blocks):
        copies[b].wait()
        for h in range(2):
            window = window_of(16 * b + 8 * h)
            mid = mid_ref[16 * b + 8 * h : 16 * b + 8 * h + 8].reshape(1024, ext)
            second = dot_nt(mid[:, :half], window[:, :half])
            second_ref[...] = second if b == 0 and h == 0 else second_ref[...] + second
            for m in range(0, 8, 2):
                store_rows(
                    window, m + 1, mid[m * 128 : m * 128 + 256], 16 * b + 8 * h + m + 1, 2
                )
    for k in range(2):
        main = jnp.where(narrow == k, beyond_ref[0].astype(f32), beside_ref[1].astype(f32))
        aside = jnp.where(narrow == k, beyond_ref[1].astype(f32), beside_ref[0].astype(f32))
        aside = jnp.where(narrow == 0, aside[:, :128], aside[:, half - 128 :])
        mask = jnp.concatenate([main, aside], axis=1)
        store_rows(window_of((rows - 8) * k), 9 * k, mask, (rows + 1) * k, 1)
    keep = pltpu.make_async_copy(masked_ref, masked_hbm, masked_sem)
    keep.start()

    amount = jnp.where(narrow == 0, 127, 1)

    def turn_in(b, into):
        for copy in in_copies[b]:
            copy.wait()
        span = slice(16 * b, 16 * b + 16)
        for z in range(2):
            turned = jnp.swapaxes(in_ref[:, z, span, :], 0, 1)
            into[1, :, z] = turned
            flat = turned.reshape(16 * channels, half).astype(f32)
            beside = jnp.swapaxes(in_side_ref[:, z, span, :], 0, 1)
            beside = pltpu.roll(beside.reshape(16 * channels, 128).astype(f32), amount, 1)
            left = flat[:, :128]
            right = flat[:, 128:]
            down_left = pltpu.roll(left, 1, 1)
            down_right = pltpu.roll(right, 1, 1)
            up_left = pltpu.roll(left, 127, 1)
            up_right = pltpu.roll(right, 127, 1)
            from_before = jnp.where(narrow == 0, 0.0, beside)
            from_after = jnp.where(narrow == 0, beside, 0.0)
            moved = {
                (0, 0): jnp.where(lane == 0, from_before, down_left),
                (0, 1): jnp.where(lane == 0, down_left, down_right),
                (2, 0): jnp.where(lane == 127, up_right, up_left),
                (2, 1): jnp.where(lane == 127, from_after, up_right),
            }
            for (d, t), value in moved.items():
                into[d, :, z, :, 128 * t : 128 * t + 128] = value.astype(bf16).reshape(
                    16, channels, 128
                )

    in_rows = (in_rows_a, in_rows_b)
    turn_in(0, in_rows[0])
    for b in range(blocks):
        if b + 1 < blocks:
            turn_in(b + 1, in_rows[(b + 1) % 2])
        held_rows = in_rows[b % 2]
        left = jnp.concatenate(
            [
                masked_ref[(16 * b + 2 * q) * 128 : (16 * b + 2 * q + 4) * 128, :half]
                for q in range(8)
            ],
            axis=1,
        )
        for d in range(3):
            right = jnp.concatenate(
                [held_rows[d, 2 * q : 2 * q + 2].reshape(256, half) for q in range(8)], axis=1
            )
            part = dot_nt(left, right)
            sum_ref[d] = part if b == 0 else sum_ref[d] + part

    singles = []
    for d in range(3):
        for dx in range(3):
            total = None
            for par in range(2):
                i4 = par + 2 - dx
                block = sum_ref[d, i4 * 128 : (i4 + 1) * 128, par * 128 : (par + 1) * 128]
                total = block if total is None else total + block
            turned = total.T
            upper = turned[:64]
            lower = turned[64:]
            slot = d * 3 + dx
            pay_ref[slot * 64 : (slot + 1) * 64] = jnp.where(lane < 64, lower, upper)
            singles.append(upper + pltpu.roll(lower, 64, 1))
    pieces = [
        second_ref[(m * 2 + z) * 64 : (m * 2 + z + 1) * 64, :] for m in range(8) for z in range(2)
    ]
    pick_copy.wait()
    second = jnp.dot(
        jnp.concatenate(pieces, axis=1), pick_ref[...].astype(f32), preferred_element_type=f32, precision=highest
    )
    singles.append(second)
    for k in range(5):
        pay_ref[(9 + k) * 64 : (10 + k) * 64] = jnp.where(
            lane < 64, singles[2 * k], pltpu.roll(singles[2 * k + 1], 64, 1)
        )
    out_ref[...] = pay_ref[...].astype(bf16)
    keep.wait()


def masked_and_kernels(
    index,
    own,
    other,
    table,
    taps,
    pick,
    beyond,
    beyond_other,
    act_in,
    in_other,
    rows_mid,
    scale,
):
    wide, held, lanes = own.shape
    rows, slices, channels, ext = rows_mid.shape
    vmem = pl.BlockSpec(memory_space=pltpu.VMEM)
    anywhere = pl.BlockSpec(memory_space=pl.ANY)
    return pl.pallas_call(
        functools.partial(masked_kernel, scale),
        out_shape=(
            pltpu.HBM(((rows + 2) * 128, ext), bf16),
            jax.ShapeDtypeStruct((14 * 64, 128), bf16),
        ),
        in_specs=[pl.BlockSpec(memory_space=pltpu.SMEM)] + [vmem] * 6 + [anywhere] * 4,
        out_specs=(anywhere, vmem),
        scratch_shapes=[
            pltpu.VMEM((14 * 64, 128), f32),
            pltpu.VMEM((3, 2, held, ext), f32),
            pltpu.VMEM((3, 512, 256), f32),
            pltpu.VMEM((1024, 128), f32),
            pltpu.VMEM(act_in.shape, bf16),
            pltpu.VMEM((channels, slices, rows, 128), bf16),
            pltpu.VMEM((3, 16, slices, channels, ext - 128), bf16),
            pltpu.VMEM((3, 16, slices, channels, ext - 128), bf16),
            pltpu.VMEM(rows_mid.shape, bf16),
            pltpu.VMEM(((rows + 2) * 128, ext), bf16),
            pltpu.VMEM(pick.shape, bf16),
            pltpu.SemaphoreType.DMA((rows // 16, 2)),
            pltpu.SemaphoreType.DMA((rows // 16,)),
            pltpu.SemaphoreType.DMA,
            pltpu.SemaphoreType.DMA,
        ],
        compiler_params=pltpu.CompilerParams(vmem_limit_bytes=48 << 20),
        name="masked_and_kernels",
    )(
        index,
        own,
        other,
        off_chip(table),
        taps,
        beyond,
        beyond_other,
        off_chip(pick),
        off_chip(act_in),
        off_chip(in_other),
        off_chip(rows_mid),
    )


def arrange_kernel(taps_ref, weight_ref):
    for dy in range(3):
        for par, i4 in ((0, 3), (1, 0)):
            weight_ref[
                par * 128 : (par + 1) * 128, dy * 512 + i4 * 128 : dy * 512 + (i4 + 1) * 128
            ] = jnp.zeros((128, 128), bf16)
        for dx in range(3):
            for z in range(2):
                tap = dx * 3 + dy
                tile = jnp.concatenate([taps_ref[(z + 1) * 9 + tap], taps_ref[z * 9 + tap]], axis=1)
                for par in range(2):
                    spot = dy * 512 + (par + 2 - dx) * 128
                    weight_ref[
                        par * 128 + z * 64 : par * 128 + (z + 1) * 64, spot : spot + 128
                    ] = tile


def arrange(w_first):
    vmem = pl.BlockSpec(memory_space=pltpu.VMEM)
    return pl.pallas_call(
        arrange_kernel,
        out_shape=jax.ShapeDtypeStruct((256, 1536), bf16),
        in_specs=[vmem],
        out_specs=vmem,
        name="arrange",
    )(w_first)


def input_kernel(base, masked_hbm, weight_ref, *rest):
    out_hbm, masked_ref, shifted_ref, wide_ref, out_ref, in_sems, out_sems = rest[-7:]
    rows = shifted_ref.shape[1] // 128 - 2
    fetches = []
    for step in range(rows // 8):
        first = 0 if step == 0 else (8 * step + 2) * 128
        last = (8 * step + 10) * 128
        fetches.append(
            pltpu.make_async_copy(
                masked_hbm.at[base * 128 + first : base * 128 + last],
                masked_ref.at[first:last],
                in_sems.at[step],
            )
        )
        fetches[step].start()
    ext = masked_ref.shape[1]
    half = ext - 128
    channels = out_ref.shape[1]
    def shift(row):
        spot = slice(row * 128, (row + 1) * 128)
        whole = masked_ref[spot, :]
        shifted_ref[1, spot, :] = whole[:, :half]
        whole = whole.astype(f32)
        for d in (0, 2):
            shifted_ref[d, spot, :] = pltpu.roll(whole, (d - 1) % ext, 1)[:, :half].astype(bf16)

    ready = 0
    outs = []
    for step in range(rows // 8):
        fetches[step].wait()
        while ready < 8 * step + 10:
            shift(ready)
            ready += 1
        for q in range(4):
            row = (8 * step + 2 * q) * 128
            stacked = jnp.concatenate(
                [shifted_ref[d, row : row + 512, :] for d in range(3)], axis=0
            )
            value = dot(weight_ref[...], stacked).astype(bf16)
            wide_ref[step % 4, 2 * q * 128 : (2 * q + 2) * 128, :] = value
        if step % 2 == 1:
            block = step // 2
            pair = jnp.concatenate([wide_ref[(step - 1) % 4], wide_ref[step % 4]], axis=0)
            pair = pair.reshape(16, 2, channels, half)
            for z in range(2):
                out_ref[block, :, z] = jnp.swapaxes(pair[:, z], 0, 1)
            first = base + 16 * block
            copy = pltpu.make_async_copy(
                out_ref.at[block], out_hbm.at[:, :, first : first + 16, :], out_sems.at[block]
            )
            copy.start()
            outs.append(copy)
    for copy in outs:
        copy.wait()


def input_gradient(masked, weight, base, rows, shape, earlier=None):
    ext = masked.shape[1]
    half = ext - 128
    channels = shape[0]
    anywhere = pl.BlockSpec(memory_space=pl.ANY)
    extra = () if earlier is None else (earlier,)
    return pl.pallas_call(
        functools.partial(input_kernel, base),
        out_shape=jax.ShapeDtypeStruct(shape, bf16),
        in_specs=[anywhere, pl.BlockSpec(memory_space=pltpu.VMEM)] + [anywhere] * len(extra),
        out_specs=anywhere,
        scratch_shapes=[
            pltpu.VMEM(((rows + 2) * 128, ext), bf16),
            pltpu.VMEM((3, (rows + 2) * 128, half), bf16),
            pltpu.VMEM((4, 1024, half), bf16),
            pltpu.VMEM((rows // 16, channels, 2, 16, half), bf16),
            pltpu.SemaphoreType.DMA((rows // 8,)),
            pltpu.SemaphoreType.DMA((rows // 16,)),
        ],
        input_output_aliases={} if earlier is None else {2: 0},
        cost_estimate=pl.CostEstimate(
            flops=2 * rows * 128 * half * 1536, bytes_accessed=4 * rows * 128 * half * 2, transcendentals=0
        ),
        compiler_params=pltpu.CompilerParams(vmem_limit_bytes=30 << 20),
        name="input_gradient",
    )(off_chip(masked), weight, *extra)


def unpack_kernel(pay_ref, first_ref, second_ref):
    slots = [pay_ref[64 * k : 64 * k + 64].astype(f32) for k in range(14)]
    for slot in range(9):
        tap = slot % 3 * 3 + slot // 3
        first_ref[18 + tap] = slots[slot][:, :64]
        first_ref[tap] = pltpu.roll(slots[slot], 64, 1)[:, :64]
        single = slots[9 + slot // 2]
        if slot % 2 == 1:
            single = pltpu.roll(single, 64, 1)
        first_ref[9 + tap] = single[:, :64]
    second_ref[...] = pltpu.roll(slots[13], 64, 1).T[:27]


def unpack(pay):
    vmem = pl.BlockSpec(memory_space=pltpu.VMEM)
    return pl.pallas_call(
        unpack_kernel,
        out_shape=(
            jax.ShapeDtypeStruct((27, 64, 64), f32),
            jax.ShapeDtypeStruct((27, 64), f32),
        ),
        in_specs=[vmem],
        out_specs=(vmem, vmem),
        name="unpack",
    )(on_chip(pay))


def tap_choice():
    choice = np.zeros((27, 10, 2, 128), np.float32)
    for dz in (-1, 0, 1):
        for dx in (-1, 0, 1):
            for dy in (-1, 0, 1):
                tap = (dz + 1) * 9 + (dx + 1) * 3 + dy + 1
                for m in range(-1, 9):
                    for z in range(2):
                        if 0 <= z - dz < 2:
                            r = m + 2 - dx
                            choice[tap, m + 1, z, ((z - dz) * 3 + dy + 1) * 16 + r] = 1
    return choice


def fast(denoised, clean_volume, weight, act_in, act_mid, w_first, w_second):
    wide = lax.axis_size("wide")
    slices, rows, half = denoised.shape
    channels = act_in.shape[0]
    keep = weight.shape[0]
    total_x = wide * rows
    total_y = 2 * half
    ext = half + 128
    narrow = lax.axis_index("narrow")
    index = narrow.astype(jnp.int32).reshape(1)
    swap = [(0, 1), (1, 0)]
    up = [(i, i + 1) for i in range(wide - 1)]
    down = [(j, i) for i, j in up]
    table_y, table_back = (jnp.asarray(t) for t in y_table(wide, keep, half))
    table_x = jnp.asarray(x_table(total_x))
    choice = tap_choice()
    pick = np.zeros((16 * 128, 128), np.float32)
    pick[:, :27] = choice[:, 1:9].reshape(27, 16 * 128).T

    error = denoised - clean_volume
    error_other = lax.ppermute(error, "narrow", swap)
    act_mid, act_in, error_other = lax.optimization_barrier((act_mid, act_in, error_other))
    mid_other = lax.ppermute(act_mid, "narrow", swap)
    in_other = lax.ppermute(act_in, "narrow", swap)
    lines = forward_y(index, error, error_other, table_y, wide)

    lines, act_mid, weight = lax.optimization_barrier((lines, act_mid, weight))
    lines = lax.all_to_all(lines, "wide", 0, 0, tiled=True)
    rows_mid, sent = turn_mid(index, act_mid, mid_other)
    ways = [(2 * i, 2 * j) for i, j in up] + [(2 * i + 1, 2 * j + 1) for i, j in down]
    beyond = lax.ppermute(sent, ("wide", "narrow"), ways)
    weight_lines = jnp.tile(weight.T, (1, 4))
    lines, weight_lines = lax.optimization_barrier((lines, weight_lines))
    lines = along_x(lines, table_x, weight_lines)

    lines, beyond, w_first, w_second = lax.optimization_barrier((lines, beyond, w_first, w_second))
    lines = lax.all_to_all(lines, "wide", 0, 0, tiled=True)
    beyond_other = lax.ppermute(beyond, "narrow", swap)
    matrix = arrange(w_first)
    taps = jnp.einsum(
        "tc,tmzk->mzck", w_second, jnp.asarray(choice, bf16), preferred_element_type=f32
    )
    taps = taps.astype(bf16).reshape(1280, 128)
    lines, matrix, taps, beyond_other = lax.optimization_barrier(
        (lines, matrix, taps, beyond_other)
    )
    lines_other = lax.ppermute(lines, "narrow", swap)
    masked, pay = masked_and_kernels(
        index,
        lines,
        lines_other,
        table_back,
        taps,
        jnp.asarray(pick, bf16),
        beyond,
        beyond_other,
        act_in,
        in_other,
        rows_mid,
        -2.0 / (total_x * total_y),
    )

    pay = pay.reshape(wide, pay.shape[0] // wide, 128)
    pay, matrix = lax.optimization_barrier((pay, matrix))
    pay = lax.all_to_all(pay, "wide", 0, 0, tiled=True)
    grad_in = input_gradient(masked, matrix, 0, rows // 2, act_in.shape)
    pay, grad_in = lax.optimization_barrier((pay, grad_in))
    total = pay.astype(f32).sum(axis=0)
    total = total + lax.ppermute(total, "narrow", swap)
    pay = jnp.broadcast_to(total.astype(bf16)[None], pay.shape)
    pay, grad_in, matrix = lax.optimization_barrier((pay, grad_in, matrix))
    pay = lax.all_to_all(pay, "wide", 0, 0, tiled=True)
    grad_in = input_gradient(masked, matrix, rows // 2, rows // 2, act_in.shape, grad_in)
    pay, grad_in = lax.optimization_barrier((pay, grad_in))
    grad_first, grad_second = unpack(pay.reshape(-1, 128))
    return (grad_in, grad_first, grad_second)


def with_halo(x, sides, width):
    for axis, dim in sides:
        devices, length = (lax.axis_size(axis), x.shape[dim])
        up = [(i, (i + 1) % devices) for i in range(devices - 1)]
        down = [(j, i) for i, j in up]
        last = lax.slice_in_dim(x, length - width, length, axis=dim)
        first = lax.slice_in_dim(x, 0, width, axis=dim)
        before = lax.ppermute(last, axis, up)
        after = lax.ppermute(first, axis, down)
        x = jnp.concatenate([before, x, after], axis=dim)
    return x


def phase_table(left_index, right_index, length):
    product = left_index[:, None] * right_index[None, :] % length
    angles = product.astype(jnp.float32) * (two_pi / length)
    return (jnp.cos(angles), jnp.sin(angles))


def shifted_windows(padded, slices, rows_x, cols_y, taps_list):
    windows = []
    for tap_index in taps_list:
        step_z = tap_index // 9 - 1
        step_x = tap_index // 3 % 3 - 1
        step_y = tap_index % 3 - 1
        windows.append(
            padded[
                ...,
                1 - step_z : 1 - step_z + slices,
                1 - step_x : 1 - step_x + rows_x,
                1 - step_y : 1 - step_y + cols_y,
            ]
        )
    return jnp.stack(windows, axis=0)


def plain(denoised, clean_volume, weight, act_in, act_mid, w_first, w_second):
    wide_count = lax.axis_size("wide")
    narrow_count = lax.axis_size("narrow")
    slices, rows_x, half_cols = denoised.shape
    total_y = half_cols * narrow_count
    total_x = rows_x * wide_count
    kept_cols = half_cols // wide_count
    narrow_index = lax.axis_index("narrow")
    error_field = denoised - clean_volume
    columns = lax.iota(jnp.int32, total_y)
    frequency = (
        columns % half_cols // kept_cols * narrow_count + columns // half_cols
    ) * kept_cols + columns % kept_cols
    own_rows = narrow_index * half_cols + lax.iota(jnp.int32, half_cols)
    cos_y, sin_y = phase_table(own_rows, frequency, total_y)
    part_real = jnp.einsum("zxy,yc->zxc", error_field, cos_y, precision=highest)
    part_imag = -jnp.einsum("zxy,yc->zxc", error_field, sin_y, precision=highest)
    spec_real, spec_imag = (
        lax.psum_scatter(part_real, "narrow", scatter_dimension=2, tiled=True),
        lax.psum_scatter(part_imag, "narrow", scatter_dimension=2, tiled=True),
    )
    positions = lax.iota(jnp.int32, total_x)
    cos_x, sin_x = phase_table(positions, positions, total_x)
    pieces = (
        lax.all_to_all(
            spec_real.reshape(slices, rows_x, wide_count, kept_cols),
            "wide",
            split_axis=2,
            concat_axis=1,
            tiled=True,
        ),
        lax.all_to_all(
            spec_imag.reshape(slices, rows_x, wide_count, kept_cols),
            "wide",
            split_axis=2,
            concat_axis=1,
            tiled=True,
        ),
    )
    item_count = pieces[0].shape[0]
    in_real = pieces[0].reshape(item_count, total_x, kept_cols)
    in_imag = pieces[1].reshape(item_count, total_x, kept_cols)
    four_real = jnp.einsum("mxk,xq->mkq", in_real, cos_x, precision=highest) + jnp.einsum(
        "mxk,xq->mkq", in_imag, sin_x, precision=highest
    )
    four_imag = jnp.einsum("mxk,xq->mkq", in_imag, cos_x, precision=highest) - jnp.einsum(
        "mxk,xq->mkq", in_real, sin_x, precision=highest
    )
    weighted_real = weight * four_real
    weighted_imag = weight * four_imag
    out_real = jnp.einsum("mkq,qx->mxk", weighted_real, cos_x, precision=highest) - jnp.einsum(
        "mkq,qx->mxk", weighted_imag, sin_x, precision=highest
    )
    out_imag = jnp.einsum("mkq,qx->mxk", weighted_imag, cos_x, precision=highest) + jnp.einsum(
        "mkq,qx->mxk", weighted_real, sin_x, precision=highest
    )
    back_real = lax.all_to_all(
        out_real.reshape(item_count, wide_count, rows_x, kept_cols),
        "wide",
        split_axis=1,
        concat_axis=3,
        tiled=True,
    ).reshape(item_count, rows_x, half_cols)
    back_imag = lax.all_to_all(
        out_imag.reshape(item_count, wide_count, rows_x, kept_cols),
        "wide",
        split_axis=1,
        concat_axis=3,
        tiled=True,
    ).reshape(item_count, rows_x, half_cols)
    local_cols = lax.iota(jnp.int32, half_cols)
    own_freq = (
        local_cols // kept_cols * narrow_count + narrow_index
    ) * kept_cols + local_cols % kept_cols
    cos_back, sin_back = phase_table(own_freq, columns, total_y)
    part_term = jnp.einsum("zxc,cy->zxy", back_real, cos_back, precision=highest) - jnp.einsum(
        "zxc,cy->zxy", back_imag, sin_back, precision=highest
    )
    field_real = lax.psum_scatter(part_term, "narrow", scatter_dimension=2, tiled=True)
    grad_noise = (field_real * (-2.0 / (total_x * total_y))).astype(jnp.bfloat16)
    noise_rim = with_halo(grad_noise, (("wide", 1), ("narrow", 2)), 1)
    noise_pad = jnp.pad(noise_rim, ((1, 1), (0, 0), (0, 0)))
    noise_windows = shifted_windows(noise_pad, slices, rows_x, half_cols, range(27))
    grad_mid = jnp.einsum(
        "tc,tzxy->czxy", w_second, noise_windows, preferred_element_type=jnp.float32
    )
    masked = jnp.where(act_mid > 0, grad_mid, 0.0).astype(jnp.bfloat16)
    masked_rim = with_halo(masked, (("wide", 2), ("narrow", 3)), 1)
    grad_second = jnp.einsum(
        "czxy,tzxy->tc", act_mid, noise_windows, preferred_element_type=jnp.float32
    )
    masked_pad = jnp.pad(masked_rim, ((0, 0), (1, 1), (0, 0), (0, 0)))
    channels = act_in.shape[0]
    grad_in = jnp.zeros(act_in.shape, jnp.float32)
    first_parts = []
    for plane_index in range(9):
        stacked = shifted_windows(
            masked_pad, slices, rows_x, half_cols, [plane_index, plane_index + 9, plane_index + 18]
        )
        first_parts.append(
            jnp.einsum("izxy,dozxy->dio", act_in, stacked, preferred_element_type=jnp.float32)
        )
        grad_in = grad_in + jnp.einsum(
            "dio,dozxy->izxy", w_first[plane_index::9], stacked, preferred_element_type=jnp.float32
        )
    grad_first = jnp.stack(first_parts, axis=1).reshape(27, channels, channels)
    grad_first, grad_second = lax.psum((grad_first, grad_second), ("wide", "narrow"))
    return (grad_in.astype(jnp.bfloat16), grad_first, grad_second)


def shards(denoised, clean_volume, weight, act_in, act_mid, w_first, w_second):
    sizes = (
        lax.axis_size("wide"),
        lax.axis_size("narrow"),
        *denoised.shape,
        weight.shape[0],
        act_in.shape[0],
    )
    chosen = fast if sizes == (8, 2, 2, 64, 256, 32, 64) else plain
    return chosen(denoised, clean_volume, weight, act_in, act_mid, w_first, w_second)


def solution(mesh):
    placed = (
        P("grp", "wide", "narrow"),
        P("grp", "wide", "narrow"),
        P(("wide", "narrow"), None),
        P(None, "grp", "wide", "narrow"),
        P(None, "grp", "wide", "narrow"),
        P(),
        P(),
    )
    return jax.shard_map(
        shards,
        mesh=mesh,
        in_specs=placed,
        out_specs=(P(None, "grp", "wide", "narrow"), P("grp", None, None), P("grp", None)),
        check_vma=False,
    )
```
